512 devices in a mesh: grp: 8 (over x, core), blk: 64 (over y, z).
Axes of the slice: x: 4, y: 8, z: 8, core: 2. Of those that a mesh axis runs over, the one named last changes fastest.
Arguments:
- features: bfloat16 [65536, 256], P(('grp', 'blk')), may hold values from -6 to 6
- dest: int32 [65536, 1], P(('grp', 'blk')), may hold values from 0 to 63; in each aligned block of 128 rows (0 to 127, 128 to 255, ...) at most 4 rows name the same one
- placement: int32 [512, 256], P(('grp', 'blk')), may hold values from 0 to 255, each once within a row
- weight: bfloat16 [27, 256, 128], replicated, may hold values from -0.078125 to 0.078125
- grad_out: bfloat16 [64, 512, 4, 128], P('grp', 'blk'), may hold values from -6 to 6
Outputs:
- output: bfloat16 [64, 512, 4, 128], P('grp', 'blk')
- grad_rows: bfloat16 [65536, 256], P(('grp', 'blk'))
- weight_grad: bfloat16 [27, 256, 128], replicated
The draws below stay inside these ranges and needn't reach their ends.
Inputs may be any that keep to these rules, and one draw needn't show every extreme that they name: `dest`: among the rows of one device no value is named by more than 4 rows, a bound that some block reaches. `placement`: each row is a permutation of 0 to 255.
All inputs are finite; a program needn't handle non-finite values.
Results may differ from the reference program's by a relative error of at most 0.0013.
Values may be sent and summed in bfloat16 or wider, within the bound.
A program may use at most 64 MiB of HBM per device.

```python
import math
import jax
import jax.numpy as jnp
import numpy as np
from jax import lax

C = 256
CO = 128
RX = 8
RY = 8
RZ = 4
VOX = 256
CAP = 4
ROWS = 128
TOTAL = 65536
NX = 64
NY = 512
N_GRP = 8
N_BLK = 64
DEVICES = 512


def shard_levels(key, extent, split, low, largest):
    level = 1.0
    for position, shards_of in split:
        draws = jax.random.uniform(jax.random.fold_in(jax.random.fold_in(key, 6), position), (shards_of,), jnp.float32, low / len(split), largest / len(split))
        level = level * jnp.repeat(jnp.exp(draws), extent[position] // shards_of).reshape((-1,) + (1,) * (len(extent) - 1 - position))
    return level


def deal_out(stream_key, own, number, rows, amount, top, reach, lean):
    order = jax.random.permutation(stream_key, amount)
    packed, usual = load_shares(amount, rows * top, reach, lean, True), load_shares(amount, rows * top, reach, lean, False)
    places = jnp.arange(amount)

    def named(tallies, offset_by):
        used = int((tallies > 0).sum())
        fixed = max(1, used // 4)
        shifted = fixed + (places - fixed + offset_by * (used - fixed)) % max(1, amount - fixed)
        return jnp.zeros((amount,), jnp.int32).at[order[jnp.where(places < fixed, places, shifted)]].set(jnp.asarray(tallies, jnp.int32))

    tallies = jnp.where(number % 4 == 0, named(packed, number // 4), named(usual, number - number // 4 - 1))
    mixed = jax.random.permutation(jax.random.fold_in(own, 3), amount)
    giver, sink = mixed[0:amount // 2 * 2:2], mixed[1:amount // 2 * 2:2]
    room = jnp.minimum(tallies[giver] - 1, reach - tallies[sink]) // 2
    room = jnp.where((giver == order[0]) | (sink == order[0]) | (tallies[sink] == 0), 0, jnp.maximum(room, 0))
    shifted = jax.random.randint(jax.random.fold_in(own, 4), (amount // 2,), 0, 1 << 20) % (room + 1)
    tallies = tallies.at[giver].add(-shifted).at[sink].add(shifted)
    items = jnp.searchsorted(jnp.cumsum(tallies), jnp.arange(rows * top), side="right").astype(jnp.int32)
    table = items.reshape(top, rows).T
    table = table[jax.random.permutation(jax.random.fold_in(own, 1), rows)]
    offset_by = jax.random.randint(jax.random.fold_in(own, 2), (rows, 1), 0, top)
    return jnp.take_along_axis(table, (jnp.arange(top)[None, :] + offset_by) % top, axis=1)


def load_shares(count, total, most, slope, full):
    weights = [(1 << 20) // math.isqrt(grade ** slope) + 1 for grade in range(1, count + 1)]
    largest = most if full else min(most, max(-(-total // count), total * weights[0] // sum(weights)))
    least = 1 if total - largest >= count - 1 else 0
    holding, spare = [largest] + [least] * (count - 1), total - largest - least * (count - 1)
    while spare > 0:
        free = [i for i in range(1, count) if holding[i] < largest] or [i for i in range(1, count) if holding[i] < most]
        mass, remaining = sum([weights[i] for i in free]), spare
        for i in free:
            more = min(most - holding[i], max(1, remaining * weights[i] // mass), spare)
            holding[i] = holding[i] + more
            spare = spare - more
    return np.array(holding)


def centred(stream_key, dims, deviation, bound, split=(), kind=jnp.bfloat16):
    level = shard_levels(stream_key, dims, split, -0.22, 0.18) if split else 1.0
    entries = jax.random.normal(stream_key, dims, jnp.float32) * deviation * level
    return jnp.minimum(jnp.maximum(entries, -bound), bound).astype(kind)


def setup_inputs(seed: int = 0) -> dict:
    seeds = jax.random.split(jax.random.key(seed), 6)
    features = centred(seeds[0], (TOTAL, C), 1.0, 6.0, ((0, 512),))
    dest_keys = jax.random.split(jax.random.fold_in(seeds[1], 1), TOTAL // ROWS)
    dest_turns = jax.random.permutation(jax.random.fold_in(seeds[1], 3), TOTAL // ROWS)
    dest = jax.vmap(lambda own, number: deal_out(jax.random.fold_in(seeds[1], 2), own, number, ROWS, N_BLK, 1, CAP, 2))(dest_keys, dest_turns).reshape((TOTAL, 1))
    placement = jax.vmap(lambda own: jax.random.permutation(own, VOX))(jax.random.split(seeds[2], DEVICES)).reshape((DEVICES, VOX)).astype(jnp.int32)
    weight = centred(seeds[3], (27, C, CO), (27 * C) ** -0.5, 0.078125)
    grad_out = centred(seeds[4], (NX, NY, RZ, CO), 1.0, 6.0, ((0, 8), (1, 64)))
    return {"features": features, "dest": dest, "placement": placement, "weight": weight, "grad_out": grad_out}


def reference(features, dest, placement, weight, grad_out):
    devices = N_GRP * N_BLK
    target = dest[:, 0].reshape(devices, ROWS)
    owners = jnp.arange(N_BLK, dtype=jnp.int32)
    one_hot = (target[:, :, None] == owners[None, None, :]).astype(jnp.int32)
    slot_rank = lax.optimization_barrier(jnp.sum((jnp.cumsum(one_hot, axis=1) - one_hot) * one_hot, axis=2))
    sender = jnp.arange(devices, dtype=jnp.int32)[:, None]
    group_index = sender // N_BLK
    block_index = sender % N_BLK
    receiver = group_index * N_BLK + target
    slot_index = block_index * CAP + slot_rank
    voxel = placement[receiver, slot_index]
    pos_x = (group_index * RX + voxel // (RY * RZ)).reshape(-1)
    pos_y = (target * RY + voxel // RZ % RY).reshape(-1)
    pos_z = (voxel % RZ).reshape(-1)
    grid = jnp.zeros((NX, NY, RZ, C), jnp.bfloat16).at[pos_x, pos_y, pos_z].set(features)
    occupied = jnp.zeros((NX, NY, RZ), jnp.float32).at[pos_x, pos_y, pos_z].set(1.0)
    occupied = occupied.reshape(-1, 1)
    count = NX * NY * RZ
    padded = jnp.pad(grid, ((1, 1), (1, 1), (1, 1), (0, 0)))
    total = jnp.zeros((count, CO), jnp.float32)
    for offset in range(27):
        shift_x, shift_y, shift_z = (offset // 9, offset // 3 % 3, offset % 3)
        window = padded[shift_x:shift_x + NX, shift_y:shift_y + NY, shift_z:shift_z + RZ].reshape(count, C)
        total = total + jnp.dot(window, weight[offset], preferred_element_type=jnp.float32)
    output = (total * occupied).astype(jnp.bfloat16).reshape(NX, NY, RZ, CO)
    masked_grad = (grad_out.reshape(count, CO).astype(jnp.float32) * occupied).astype(jnp.bfloat16)
    grad_padded = jnp.pad(masked_grad.reshape(NX, NY, RZ, CO), ((1, 1), (1, 1), (1, 1), (0, 0)))
    back_total = jnp.zeros((count, C), jnp.float32)
    partials = []
    for offset in range(27):
        shift_x, shift_y, shift_z = (offset // 9, offset // 3 % 3, offset % 3)
        window = grad_padded[2 - shift_x:2 - shift_x + NX, 2 - shift_y:2 - shift_y + NY, 2 - shift_z:2 - shift_z + RZ].reshape(count, CO)
        back_total = back_total + lax.dot_general(window, weight[offset], (((1,), (1,)), ((), ())), preferred_element_type=jnp.float32)
        source = padded[shift_x:shift_x + NX, shift_y:shift_y + NY, shift_z:shift_z + RZ].reshape(count, C)
        partials.append(lax.dot_general(source, masked_grad, (((0,), (0,)), ((), ())), preferred_element_type=jnp.float32))
    grad_grid = (back_total * occupied).astype(jnp.bfloat16).reshape(NX, NY, RZ, C)
    grad_scale = 1.0 / math.sqrt(ROWS * N_GRP * N_BLK)
    weight_grad = (jnp.stack(partials) * grad_scale).astype(jnp.bfloat16)
    grad_rows = grad_grid[pos_x, pos_y, pos_z]
    return (output, grad_rows, weight_grad)
```

```python
import functools
import math

import jax
import jax.numpy as jnp
from jax import lax
from jax.experimental import pallas as pl
from jax.experimental.pallas import tpu as pltpu
from jax.sharding import PartitionSpec as P

MESH = pl.DeviceIdType.MESH
F32, BF16 = jnp.float32, jnp.bfloat16
SIZES = {"x": 4, "y": 8, "z": 8}
PARTS = ((0, 11, "xyz"), (11, 8, "yzx"), (19, 8, "zxy"))
TILE = (8, 128)


def part_sizes(part):
    first, count, axes = part
    na, nb, nc = (SIZES[a] for a in axes)
    per_core = count * 32 // 2
    n_a = per_core // na
    n_b = -(-n_a // nb)
    return na, nb, nc, per_core, n_a, n_b


def reduce_scratch():
    shapes = []
    for part in PARTS:
        na, nb, nc, per_core, n_a, n_b = part_sizes(part)
        shapes += [
            pltpu.VMEM((na, n_a) + TILE, F32),
            pltpu.VMEM((na - 1, n_a) + TILE, F32),
            pltpu.VMEM((nb * n_b,) + TILE, F32),
            pltpu.VMEM((nb - 1, n_b) + TILE, F32),
            pltpu.VMEM((nc, n_b) + TILE, F32),
            pltpu.VMEM((nb * n_b,) + TILE, BF16),
        ]
        for n in (na, na, nb, nc, nb, na, na):
            shapes += [pltpu.SemaphoreType.DMA((n,)), pltpu.SemaphoreType.DMA((n,))]
    return shapes


PER_PART = 6 + 14


def coords():
    g, b = lax.axis_index("grp"), lax.axis_index("blk")
    return {"x": g // 2, "c": g % 2, "y": b // 8, "z": b % 8}


def device(at, axis, value):
    at = dict(at)
    at[axis] = value
    return (at["x"] * 2 + at["c"], at["y"] * 8 + at["z"])


def greet(at):
    peers = [device(at, "c", 1 - at["c"])]
    for axis, n in SIZES.items():
        peers += [device(at, axis, (at[axis] + r) % n) for r in range(1, n)]
    return peers


def reduce_steps(at, scale, p_ref, out_ref, scratch):
    c = at["c"]
    sibling = device(at, "c", 1 - c)
    plans = []
    for i, part in enumerate(PARTS):
        own = scratch[i * PER_PART : (i + 1) * PER_PART]
        plans.append((part, part_sizes(part), own[:6], own[6:]))
    sends = []

    def copy(src, dst, send, recv, who):
        made = pltpu.make_async_remote_copy(
            src_ref=src, dst_ref=dst, send_sem=send, recv_sem=recv, device_id=who, device_id_type=MESH
        )
        made.start()
        sends.append(made)
        return made

    def chunk(plan, core, r):
        (first, _, axes), (na, nb, nc, per_core, n_a, n_b), _, _ = plan
        return pl.ds(first * 32 + core * per_core + (at[axes[0]] + r) % na * n_a, n_a)

    rounds = [(r, plan) for r in list(range(1, 8)) + [0] for plan in plans if r < plan[1][0]]
    core_copies = {}
    for r, plan in rounds:
        bufs, sems = plan[2], plan[3]
        core_copies[r, plan[0]] = copy(
            p_ref.at[chunk(plan, 1 - c, r)], bufs[0].at[r], sems[0].at[r], sems[1].at[r], sibling
        )
    a_copies = {}
    for r, plan in rounds:
        (first, _, axes), (na, *_), bufs, sems = plan
        core_copies[r, plan[0]].wait_recv()
        bufs[0][r] = bufs[0][r] + p_ref[chunk(plan, c, r)]
        if r:
            who = device(at, axes[0], (at[axes[0]] + r) % na)
            a_copies[r, plan[0]] = copy(bufs[0].at[r], bufs[1].at[r - 1], sems[2].at[r], sems[3].at[r], who)
    yield
    b_copies = {}
    for plan in plans:
        (first, _, axes), (na, nb, nc, per_core, n_a, n_b), bufs, sems = plan
        total = bufs[0][0]
        for r in range(1, na):
            a_copies[r, plan[0]].wait_recv()
            total = total + bufs[1][r - 1]
        bufs[2][pl.ds(0, n_a)] = total
        if n_a < nb * n_b:
            bufs[2][pl.ds(n_a, nb * n_b - n_a)] = jnp.zeros((nb * n_b - n_a,) + TILE, F32)
        me = at[axes[1]]
        for r in range(1, nb):
            to = (me + r) % nb
            b_copies[r, plan[0]] = copy(
                bufs[2].at[pl.ds(to * n_b, n_b)], bufs[3].at[r - 1], sems[4].at[r], sems[5].at[r], device(at, axes[1], to)
            )
    yield
    c_copies = {}
    for plan in plans:
        (first, _, axes), (na, nb, nc, per_core, n_a, n_b), bufs, sems = plan
        total = bufs[2][pl.ds(at[axes[1]] * n_b, n_b)]
        for r in range(1, nb):
            b_copies[r, plan[0]].wait_recv()
            total = total + bufs[3][r - 1]
        me = at[axes[2]]
        bufs[4][me] = total
        for r in range(1, nc):
            to = (me + r) % nc
            c_copies[r, plan[0]] = copy(bufs[4].at[me], bufs[4].at[me], sems[6].at[r], sems[7].at[r], device(at, axes[2], to))
    yield
    g_copies = {}
    for plan in plans:
        (first, _, axes), (na, nb, nc, per_core, n_a, n_b), bufs, sems = plan
        for r in range(1, nc):
            c_copies[r, plan[0]].wait_recv()
        total = bufs[4][0]
        for i in range(1, nc):
            total = total + bufs[4][i]
        me = at[axes[1]]
        mine = pl.ds(me * n_b, n_b)
        bufs[5][mine] = (total * scale).astype(BF16)
        for r in range(1, nb):
            to = (me + r) % nb
            g_copies[r, plan[0]] = copy(bufs[5].at[mine], bufs[5].at[mine], sems[8].at[r], sems[9].at[r], device(at, axes[1], to))
    yield
    o_copies, f_copies = {}, []
    for plan in plans:
        (first, _, axes), (na, nb, nc, per_core, n_a, n_b), bufs, sems = plan
        for r in range(1, nb):
            g_copies[r, plan[0]].wait_recv()
        mine = chunk(plan, c, 0)
        out_ref[mine] = bufs[5][pl.ds(0, n_a)]
        whole = bufs[5].at[pl.ds(0, n_a)]
        for r in range(1, na):
            to = (at[axes[0]] + r) % na
            o_copies[r, plan[0]] = copy(whole, out_ref.at[mine], sems[10].at[r], sems[11].at[r], device(at, axes[0], to))
        f_copies.append(copy(whole, out_ref.at[mine], sems[12].at[0], sems[13].at[0], sibling))
    for r in range(1, 8):
        for plan in plans:
            na, bufs, sems = plan[1][0], plan[2], plan[3]
            if r < na:
                o_copies[r, plan[0]].wait_recv()
                came = out_ref.at[chunk(plan, c, na - r)]
                f_copies.append(copy(came, came, sems[12].at[r], sems[13].at[r], sibling))
    yield
    for made in f_copies:
        made.wait_recv()
    for made in sends:
        made.wait_send()


def kernel(scale, p_ref, out_ref, *scratch):
    at = coords()
    barrier = pltpu.get_barrier_semaphore()
    peers = greet(at)
    for who in peers:
        pl.semaphore_signal(barrier, inc=1, device_id=who, device_id_type=MESH)
    pl.semaphore_wait(barrier, len(peers))
    for _ in reduce_steps(at, scale, p_ref, out_ref, scratch):
        pass


def all_reduce(p, scale):
    return pl.pallas_call(
        functools.partial(kernel, scale),
        out_shape=jax.ShapeDtypeStruct((864, 8, 128), BF16),
        in_specs=[pl.BlockSpec(memory_space=pltpu.VMEM)],
        out_specs=pl.BlockSpec(memory_space=pltpu.VMEM),
        scratch_shapes=reduce_scratch(),
        compiler_params=pltpu.CompilerParams(collective_id=2, has_side_effects=True, vmem_limit_bytes=40 << 20),
    )(p)


def extended(cells, sides, width):
    for axis, dim in sides:
        count = lax.axis_size(axis)
        ends = count - 1
        head = lax.slice_in_dim(cells, 0, width, axis=dim)
        tail = lax.slice_in_dim(cells, cells.shape[dim] - width, cells.shape[dim], axis=dim)
        cells = jnp.concatenate(
            [
                lax.ppermute(tail, axis, [(i, (i + 1) % count) for i in range(ends)]),
                cells,
                lax.ppermute(head, axis, [((i + 1) % count, i) for i in range(ends)]),
            ],
            axis=dim,
        )
    return cells


def shards(features, dest, placement, weight, grad_out):
    row_count, channels = features.shape
    blk_count = lax.axis_size("blk")
    grp_count = lax.axis_size("grp")
    voxel_of_slot = placement[0]
    voxel_count = voxel_of_slot.shape[0]
    capacity = voxel_count // blk_count
    size_x, size_y, size_z, out_channels = grad_out.shape
    target = dest[:, 0]
    owners = jnp.arange(blk_count, dtype=jnp.int32)
    one_hot = (target[:, None] == owners[None, :]).astype(jnp.int32)
    order = jnp.arange(row_count, dtype=jnp.int32)
    earlier = (target[:, None] == target[None, :]) & (order[None, :] < order[:, None])
    slot_rank = jnp.sum(earlier.astype(jnp.int32), axis=1)
    send_counts = jnp.sum(one_hot, axis=0).reshape(blk_count, 1)
    slot_index = target * capacity + slot_rank
    outgoing = jnp.zeros((voxel_count, channels), jnp.bfloat16).at[slot_index].set(features)
    incoming, recv_counts = (
        lax.all_to_all(
            outgoing.reshape(blk_count, capacity, channels),
            "blk",
            split_axis=0,
            concat_axis=0,
            tiled=True,
        ),
        lax.all_to_all(send_counts, "blk", split_axis=0, concat_axis=0, tiled=True),
    )
    filled = (
        (jnp.arange(capacity, dtype=jnp.int32)[None, :] < recv_counts)
        .reshape(-1)
        .astype(jnp.float32)
    )
    voxel_rows = (
        jnp.zeros((voxel_count, channels), jnp.bfloat16)
        .at[voxel_of_slot]
        .set(incoming.reshape(voxel_count, channels))
    )
    occupied = jnp.zeros((voxel_count,), jnp.float32).at[voxel_of_slot].set(filled)[:, None]
    voxel_grid = voxel_rows.reshape(size_x, size_y, size_z, channels)
    padded = extended(voxel_grid, (("grp", 0), ("blk", 1)), 1)
    padded = jnp.pad(padded, ((0, 0), (0, 0), (1, 1), (0, 0)))
    shifted = []
    total = jnp.zeros((voxel_count, out_channels), jnp.float32)
    for offset in range(27):
        shift_x, shift_y, shift_z = (offset // 9, offset // 3 % 3, offset % 3)
        window = padded[
            shift_x : shift_x + size_x, shift_y : shift_y + size_y, shift_z : shift_z + size_z
        ].reshape(voxel_count, channels)
        shifted.append(window)
        total = total + jnp.dot(window, weight[offset], preferred_element_type=jnp.float32)
    output = (total * occupied).astype(jnp.bfloat16).reshape(size_x, size_y, size_z, out_channels)
    masked_grad = (
        grad_out.reshape(voxel_count, out_channels).astype(jnp.float32) * occupied
    ).astype(jnp.bfloat16)
    grad_padded = extended(
        masked_grad.reshape(size_x, size_y, size_z, out_channels), (("grp", 0), ("blk", 1)), 1
    )
    grad_padded = jnp.pad(grad_padded, ((0, 0), (0, 0), (1, 1), (0, 0)))
    back_total = jnp.zeros((voxel_count, channels), jnp.float32)
    partials = []
    for offset in range(27):
        shift_x, shift_y, shift_z = (offset // 9, offset // 3 % 3, offset % 3)
        window = grad_padded[
            2 - shift_x : 2 - shift_x + size_x,
            2 - shift_y : 2 - shift_y + size_y,
            2 - shift_z : 2 - shift_z + size_z,
        ].reshape(voxel_count, out_channels)
        back_total = back_total + lax.dot_general(
            window, weight[offset], (((1,), (1,)), ((), ())), preferred_element_type=jnp.float32
        )
        partials.append(
            lax.dot_general(
                shifted[offset],
                masked_grad,
                (((0,), (0,)), ((), ())),
                preferred_element_type=jnp.float32,
            )
        )
    grad_grid = (back_total * occupied).astype(jnp.bfloat16)
    weight_terms = jnp.stack(partials).reshape(27 * channels // 8, 8, out_channels)
    grad_scale = 1.0 / math.sqrt(row_count * blk_count * grp_count)
    weight_grad = all_reduce(weight_terms, grad_scale).reshape(27, channels, out_channels)
    returning = grad_grid[voxel_of_slot].reshape(blk_count, capacity, channels)
    returned = lax.all_to_all(returning, "blk", split_axis=0, concat_axis=0, tiled=True)
    grad_rows = returned.reshape(voxel_count, channels)[slot_index]
    return (output, grad_rows, weight_grad)


def solution(mesh):
    in_specs = (
        P(("grp", "blk"), None),
        P(("grp", "blk"), None),
        P(("grp", "blk"), None),
        P(),
        P("grp", "blk", None, None),
    )
    out_specs = (P("grp", "blk", None, None), P(("grp", "blk"), None), P())
    return jax.shard_map(shards, mesh=mesh, in_specs=in_specs, out_specs=out_specs, check_vma=False)
```

```python
import functools
import math

import jax
import jax.numpy as jnp
from jax import lax
from jax.experimental import pallas as pl
from jax.experimental.pallas import tpu as pltpu
from jax.sharding import PartitionSpec as P

MESH = pl.DeviceIdType.MESH
F32, BF16 = jnp.float32, jnp.bfloat16
SIZES = {"x": 4, "y": 8, "z": 8}
PARTS = ((0, 11, "xyz"), (11, 8, "yzx"), (19, 8, "zxy"))
TILE = (8, 128)


def part_sizes(part):
    first, count, axes = part
    na, nb, nc = (SIZES[a] for a in axes)
    per_core = count * 32 // 2
    n_a = per_core // na
    n_b = -(-n_a // nb)
    return na, nb, nc, per_core, n_a, n_b


def reduce_scratch():
    shapes = []
    for part in PARTS:
        na, nb, nc, per_core, n_a, n_b = part_sizes(part)
        shapes += [
            pltpu.VMEM((na, n_a) + TILE, F32),
            pltpu.VMEM((na - 1, n_a) + TILE, F32),
            pltpu.VMEM((nb * n_b,) + TILE, F32),
            pltpu.VMEM((nb - 1, n_b) + TILE, F32),
            pltpu.VMEM((nc, n_b) + TILE, F32),
            pltpu.VMEM((nb * n_b,) + TILE, BF16),
        ]
        for n in (na, na, nb, nc, nb, na, na):
            shapes += [pltpu.SemaphoreType.DMA((n,)), pltpu.SemaphoreType.DMA((n,))]
    return shapes


PER_PART = 6 + 14


def coords():
    g, b = lax.axis_index("grp"), lax.axis_index("blk")
    return {"x": g // 2, "c": g % 2, "y": b // 8, "z": b % 8}


def device(at, axis, value):
    at = dict(at)
    at[axis] = value
    return (at["x"] * 2 + at["c"], at["y"] * 8 + at["z"])


def reduce_steps(at, scale, p_ref, out_ref, scratch):
    c = at["c"]
    sibling = device(at, "c", 1 - c)
    plans = []
    for i, part in enumerate(PARTS):
        own = scratch[i * PER_PART : (i + 1) * PER_PART]
        plans.append((part, part_sizes(part), own[:6], own[6:]))
    sends = []

    def copy(src, dst, send, recv, who):
        made = pltpu.make_async_remote_copy(
            src_ref=src, dst_ref=dst, send_sem=send, recv_sem=recv, device_id=who, device_id_type=MESH
        )
        made.start()
        sends.append(made)
        return made

    def chunk(plan, core, r):
        (first, _, axes), (na, nb, nc, per_core, n_a, n_b), _, _ = plan
        return pl.ds(first * 32 + core * per_core + (at[axes[0]] + r) % na * n_a, n_a)

    rounds = [(r, plan) for r in list(range(1, 8)) + [0] for plan in plans if r < plan[1][0]]
    core_copies = {}
    for r, plan in rounds:
        bufs, sems = plan[2], plan[3]
        core_copies[r, plan[0]] = copy(
            p_ref.at[chunk(plan, 1 - c, r)], bufs[0].at[r], sems[0].at[r], sems[1].at[r], sibling
        )
    a_copies = {}
    for r, plan in rounds:
        (first, _, axes), (na, *_), bufs, sems = plan
        core_copies[r, plan[0]].wait_recv()
        bufs[0][r] = bufs[0][r] + p_ref[chunk(plan, c, r)]
        if r:
            who = device(at, axes[0], (at[axes[0]] + r) % na)
            a_copies[r, plan[0]] = copy(bufs[0].at[r], bufs[1].at[r - 1], sems[2].at[r], sems[3].at[r], who)
    yield
    b_copies = {}
    for plan in plans:
        (first, _, axes), (na, nb, nc, per_core, n_a, n_b), bufs, sems = plan
        total = bufs[0][0]
        for r in range(1, na):
            a_copies[r, plan[0]].wait_recv()
            total = total + bufs[1][r - 1]
        bufs[2][pl.ds(0, n_a)] = total
        if n_a < nb * n_b:
            bufs[2][pl.ds(n_a, nb * n_b - n_a)] = jnp.zeros((nb * n_b - n_a,) + TILE, F32)
        me = at[axes[1]]
        for r in range(1, nb):
            to = (me + r) % nb
            b_copies[r, plan[0]] = copy(
                bufs[2].at[pl.ds(to * n_b, n_b)], bufs[3].at[r - 1], sems[4].at[r], sems[5].at[r], device(at, axes[1], to)
            )
    yield
    c_copies = {}
    for plan in plans:
        (first, _, axes), (na, nb, nc, per_core, n_a, n_b), bufs, sems = plan
        total = bufs[2][pl.ds(at[axes[1]] * n_b, n_b)]
        for r in range(1, nb):
            b_copies[r, plan[0]].wait_recv()
            total = total + bufs[3][r - 1]
        me = at[axes[2]]
        bufs[4][me] = total
        for r in range(1, nc):
            to = (me + r) % nc
            c_copies[r, plan[0]] = copy(bufs[4].at[me], bufs[4].at[me], sems[6].at[r], sems[7].at[r], device(at, axes[2], to))
    yield
    g_copies = {}
    for plan in plans:
        (first, _, axes), (na, nb, nc, per_core, n_a, n_b), bufs, sems = plan
        for r in range(1, nc):
            c_copies[r, plan[0]].wait_recv()
        total = bufs[4][0]
        for i in range(1, nc):
            total = total + bufs[4][i]
        me = at[axes[1]]
        mine = pl.ds(me * n_b, n_b)
        bufs[5][mine] = (total * scale).astype(BF16)
        for r in range(1, nb):
            to = (me + r) % nb
            g_copies[r, plan[0]] = copy(bufs[5].at[mine], bufs[5].at[mine], sems[8].at[r], sems[9].at[r], device(at, axes[1], to))
    yield
    o_copies, f_copies = {}, []
    for plan in plans:
        (first, _, axes), (na, nb, nc, per_core, n_a, n_b), bufs, sems = plan
        for r in range(1, nb):
            g_copies[r, plan[0]].wait_recv()
        mine = chunk(plan, c, 0)
        out_ref[mine] = bufs[5][pl.ds(0, n_a)]
        whole = bufs[5].at[pl.ds(0, n_a)]
        for r in range(1, na):
            to = (at[axes[0]] + r) % na
            o_copies[r, plan[0]] = copy(whole, out_ref.at[mine], sems[10].at[r], sems[11].at[r], device(at, axes[0], to))
        f_copies.append(copy(whole, out_ref.at[mine], sems[12].at[0], sems[13].at[0], sibling))
    for r in range(1, 8):
        for plan in plans:
            na, bufs, sems = plan[1][0], plan[2], plan[3]
            if r < na:
                o_copies[r, plan[0]].wait_recv()
                came = out_ref.at[chunk(plan, c, na - r)]
                f_copies.append(copy(came, came, sems[12].at[r], sems[13].at[r], sibling))
    yield
    for made in f_copies:
        made.wait_recv()
    for made in sends:
        made.wait_send()


VOX, SLOTS, ROWS = 256, 512, 128
GRP, BLK = 8, 64
HALO = 160
BLOCKS = ((0, 4), (4, 4), (8, 4), (12, 4), (16, 1), (17, 1), (18, 1), (19, 1))
SIDES = ((-1, 0), (1, 0), (0, -1), (0, 1), (-1, -1), (-1, 1), (1, -1), (1, 1))


def iota(shape, dim):
    return lax.broadcasted_iota(jnp.int32, shape, dim)


def dot(a, b, dims=((1,), (0,))):
    return lax.dot_general(a, b, (dims, ((), ())), preferred_element_type=F32)


def one(mask):
    return jnp.where(mask, 1.0, 0.0).astype(BF16)


def inner(v):
    return (v & 3) * 64 + (v >> 5) * 8 + ((v >> 2) & 7)


def row_slots(dest_col, by_row):
    wide = jnp.broadcast_to(dest_col, (ROWS, ROWS))
    turned = wide.astype(F32).T.astype(jnp.int32)
    i, j = iota((ROWS, ROWS), 0), iota((ROWS, ROWS), 1)
    same = wide == turned
    if by_row:
        rank = jnp.sum(jnp.where(same & (j < i), 1.0, 0.0), axis=1, keepdims=True)
        return dest_col * 8 + rank.astype(jnp.int32)
    rank = jnp.sum(jnp.where(same & (i < j), 1.0, 0.0), axis=0, keepdims=True)
    return turned[0:1] * 8 + rank.astype(jnp.int32)


def spread(shape, slot_dim):
    slot, half = iota(shape, slot_dim), iota(shape, 1 - slot_dim)
    return one((half >> 3) * 4 + (half & 3) == slot)


def face_source(row):
    t = row & 31
    far = jnp.where((row & 32) != 0, 7, 0)
    x_side = (t >> 3) * 64 + far * 8 + (t & 7)
    y_side = (t >> 3) * 64 + (t & 7) * 8 + far
    k = (row - 128) >> 3
    corner = (row & 3) * 64 + (k >> 1) * 56 + (k & 1) * 7
    return jnp.where(row < 64, x_side, jnp.where(row < 128, y_side, corner))


def cell_source(row, shift_y):
    z = row // 80
    x = (row >> 3) - z * 10 - 1
    y = (row & 7) + (shift_y - 1)
    in_x, in_y = (x >= 0) & (x < 8), (y >= 0) & (y < 8)
    right, top = jnp.where(x > 7, 1, 0), jnp.where(y > 7, 1, 0)
    inside = z * 64 + x * 8 + y
    x_side = VOX + right * 32 + z * 8 + y
    y_side = VOX + 64 + top * 32 + z * 8 + x
    corner = VOX + 128 + right * 16 + top * 8 + z
    return jnp.where(in_x & in_y, inside, jnp.where(in_y, x_side, jnp.where(in_x, y_side, corner)))


def greet_block(barrier, g, b):
    def signal(r, _):
        pl.semaphore_signal(barrier, inc=1, device_id=(g, (b + r) % BLK), device_id_type=MESH)
        return 0

    lax.fori_loop(1, BLK, signal, 0)


def start_all_to_all(g, b, out_ref, in_ref, sems):
    def send(r, _):
        to = (b + r) % BLK
        pltpu.make_async_remote_copy(
            src_ref=out_ref.at[to],
            dst_ref=in_ref.at[b],
            send_sem=sems.at[0],
            recv_sem=sems.at[1],
            device_id=(g, to),
            device_id_type=MESH,
        ).start()
        return 0

    lax.fori_loop(1, BLK, send, 0)


def end_all_to_all(g, b, out_ref, in_ref, sems):
    pltpu.make_async_remote_copy(
        src_ref=out_ref.at[pl.ds(0, BLK - 1)],
        dst_ref=in_ref.at[pl.ds(0, BLK - 1)],
        send_sem=sems.at[0],
        recv_sem=sems.at[1],
        device_id=(g, (b + 1) % BLK),
        device_id_type=MESH,
    ).wait()


def exchange_kernel(dest_ref, features_ref, place_ref, grad_ref, own_ref, halo_ref, out, came, face, edge, sems, send_sems, recv_sems):
    g, b = lax.axis_index("grp"), lax.axis_index("blk")
    barrier = pltpu.get_barrier_semaphore()
    greet_block(barrier, g, b)
    for dx in (-1, 1):
        for dy in (-1, 0, 1):
            who = ((g + dx + GRP) % GRP, (b + dy + BLK) % BLK)
            pl.semaphore_signal(barrier, inc=1, device_id=who, device_id_type=MESH)

    slot = row_slots(dest_ref[...], False)
    half = iota((SLOTS, ROWS), 0)
    first, second = half == slot, half == slot + 4
    packed = dot(one(first), features_ref[:, :128]) + dot(one(second), features_ref[:, 128:])
    held = dot(one(first | second), jnp.ones((ROWS, 128), BF16))
    out[...] = jnp.where(held > 0.5, packed, jnp.inf).reshape(BLK, 8, 128).astype(BF16)
    pl.semaphore_wait(barrier, BLK - 1 + 6)
    start_all_to_all(g, b, out, came, sems)
    came[b] = out[b]

    places = jnp.broadcast_to(place_ref[...], (8, VOX)).astype(F32).astype(BF16)
    place8 = dot(places, spread((VOX, SLOTS), 0))[0:1].astype(jnp.int32)
    hits = iota((VOX, SLOTS), 0) == inner(place8)
    low = (iota((VOX, SLOTS), 1) & 4) == 0
    low_hits, high_hits = one(hits & low), one(hits & ~low)
    order = one(inner(iota((VOX, VOX), 1)) == iota((VOX, VOX), 0))
    grad = dot(order, grad_ref[...])
    face_of = one(face_source(iota((HALO, VOX), 0)) == iota((HALO, VOX), 1))

    end_all_to_all(g, b, out, came, sems)
    got = came[...].astype(F32).reshape(SLOTS, 128)
    there = got < jnp.inf
    rows = jnp.where(there, got, 0.0).astype(BF16)
    left = dot(low_hits, rows).astype(BF16)
    right = dot(high_hits, rows).astype(BF16)
    occupied = dot(low_hits, one(there))
    masked = (grad * occupied).astype(BF16)
    cells = jnp.concatenate([left, right, masked], axis=1)
    own_ref[:, 0:384] = cells
    own_ref[:, 384:512] = occupied.astype(BF16)
    face[...] = dot(face_of, cells).reshape(HALO // 8, 8, 384).astype(BF16)
    copies = []
    for k, ((at, size), (dx, dy)) in enumerate(zip(BLOCKS, SIDES)):
        back = SIDES.index((-dx, -dy))
        made = pltpu.make_async_remote_copy(
            src_ref=face.at[pl.ds(at, size)],
            dst_ref=edge.at[pl.ds(BLOCKS[back][0], size)],
            send_sem=send_sems.at[k],
            recv_sem=recv_sems.at[k],
            device_id=((g + dx + GRP) % GRP, (b + dy + BLK) % BLK),
            device_id_type=MESH,
        )
        made.start()
        copies.append(made)
    row = iota((HALO, 1), 0)
    k = (row - 128) >> 3
    on_x = (row < 64) | (row >= 128)
    on_y = row >= 64
    x_far = jnp.where(row < 64, row >> 5, k >> 1)
    y_far = jnp.where(row < 128, (row - 64) >> 5, k & 1)
    at_x = jnp.where(x_far == 1, jnp.where(g == GRP - 1, 1, 0), jnp.where(g == 0, 1, 0))
    at_y = jnp.where(y_far == 1, jnp.where(b == BLK - 1, 1, 0), jnp.where(b == 0, 1, 0))
    beyond_x = on_x & (at_x == 1)
    beyond_y = on_y & (at_y == 1)
    beyond = beyond_x | beyond_y
    for made in copies:
        made.wait()
    halo = edge[...].astype(F32).reshape(HALO, 384)
    halo_ref[...] = jnp.where(beyond, 0.0, halo).astype(BF16)


def exchange(dest, features, placement, grad_out):
    vmem = pl.BlockSpec(memory_space=pltpu.VMEM)
    return pl.pallas_call(
        exchange_kernel,
        out_shape=(jax.ShapeDtypeStruct((VOX, 512), BF16), jax.ShapeDtypeStruct((HALO, 384), BF16)),
        in_specs=[vmem] * 4,
        out_specs=(vmem, vmem),
        scratch_shapes=[
            pltpu.VMEM((BLK, 8, 128), BF16),
            pltpu.VMEM((BLK, 8, 128), BF16),
            pltpu.VMEM((HALO // 8, 8, 384), BF16),
            pltpu.VMEM((HALO // 8, 8, 384), BF16),
            pltpu.SemaphoreType.DMA((2,)),
            pltpu.SemaphoreType.DMA((8,)),
            pltpu.SemaphoreType.DMA((8,)),
        ],
        compiler_params=pltpu.CompilerParams(collective_id=1, has_side_effects=True, vmem_limit_bytes=24 << 20),
    )(dest, features, placement, grad_out)


def convolve_kernel(own_ref, halo_ref, weight_ref, place_ref, terms_ref, output_ref, back_ref, cells_f, cells_g):
    data = jnp.concatenate([own_ref[:, :384], halo_ref[...]], axis=0)
    for y in range(3):
        select = one(cell_source(iota((320, 1), 0), y) == iota((320, VOX + HALO), 1))
        moved = dot(select, data)
        for ref, part in ((cells_f, moved[:, :256]), (cells_g, moved[:, 256:])):
            lanes = part.shape[1]
            ref[y, 1:5] = part.reshape(4, 10, 8, lanes)
            ref[y, 0] = jnp.zeros((10, 8, lanes), F32)
            ref[y, 5] = jnp.zeros((10, 8, lanes), F32)
    turned = own_ref[:, :256].astype(F32).T.astype(BF16)
    total = jnp.zeros((VOX, 128), F32)
    back = jnp.zeros((VOX, 256), F32)

    def window(ref, x, y, z):
        part = ref[y, z : z + 4, x : x + 8]
        return part.reshape(VOX, part.shape[-1]).astype(BF16)

    for x in range(3):
        for y in range(3):
            k = x * 9 + y * 3
            seen = jnp.concatenate([window(cells_g, 2 - x, 2 - y, 2 - z) for z in range(3)], axis=1)
            terms = dot(turned, seen)
            for z in range(3):
                terms_ref[(k + z) * 32 : (k + z + 1) * 32] = terms[:, z * 128 : (z + 1) * 128].reshape(32, 8, 128)
            flat = jnp.concatenate([weight_ref[k + z] for z in range(3)], axis=1)
            back = back + dot(seen, flat, ((1,), (1,)))
            near = jnp.concatenate([window(cells_f, x, y, z) for z in range(3)], axis=1)
            tall = jnp.concatenate([weight_ref[k + z] for z in range(3)], axis=0)
            total = total + dot(near, tall)
    occupied = own_ref[:, 384:512].astype(F32)
    order = one(inner(iota((VOX, VOX), 0)) == iota((VOX, VOX), 1))
    output_ref[...] = dot(order, (total * occupied).astype(BF16)).astype(BF16)
    grid_l = (back[:, :128] * occupied).astype(BF16)
    grid_r = (back[:, 128:] * occupied).astype(BF16)
    places = jnp.broadcast_to(place_ref[...], (8, VOX)).astype(F32).astype(BF16)
    place8 = dot(spread((SLOTS, VOX), 1), places, ((1,), (1,)))[:, 0:1].astype(jnp.int32)
    hits = inner(place8) == iota((SLOTS, VOX), 1)
    low = (iota((SLOTS, VOX), 0) & 4) == 0
    sent = dot(one(hits & low), grid_l) + dot(one(hits & ~low), grid_r)
    back_ref[...] = sent.reshape(BLK, 8, 128).astype(BF16)


def convolve(own, halo, weight, placement):
    vmem = pl.BlockSpec(memory_space=pltpu.VMEM)
    return pl.pallas_call(
        convolve_kernel,
        out_shape=(
            jax.ShapeDtypeStruct((864, 8, 128), F32),
            jax.ShapeDtypeStruct((VOX, 128), BF16),
            jax.ShapeDtypeStruct((BLK, 8, 128), BF16),
        ),
        in_specs=[vmem] * 4,
        out_specs=(vmem,) * 3,
        scratch_shapes=[pltpu.VMEM((3, 6, 10, 8, 256), F32), pltpu.VMEM((3, 6, 10, 8, 128), F32)],
        compiler_params=pltpu.CompilerParams(vmem_limit_bytes=40 << 20),
    )(own, halo, weight, placement)


def finish_kernel(scale, terms_ref, back_ref, dest_ref, out_ref, rows_ref, came, sems, *scratch):
    g, b = lax.axis_index("grp"), lax.axis_index("blk")
    at = coords()
    barrier = pltpu.get_barrier_semaphore()
    greet_block(barrier, g, b)
    peers = [device(at, "c", 1 - at["c"])] + [device(at, "x", (at["x"] + r) % 4) for r in range(1, 4)]
    for who in peers:
        pl.semaphore_signal(barrier, inc=1, device_id=who, device_id_type=MESH)
    pl.semaphore_wait(barrier, BLK - 1 + len(peers))
    steps = reduce_steps(at, scale, terms_ref, out_ref, scratch)
    next(steps)
    start_all_to_all(g, b, back_ref, came, sems)
    came[b] = back_ref[b]
    slot = row_slots(dest_ref[...], True)
    half = iota((ROWS, SLOTS), 1)
    low, high = one(half == slot), one(half == slot + 4)
    next(steps)
    end_all_to_all(g, b, back_ref, came, sems)
    rows = came[...].astype(F32).reshape(SLOTS, 128).astype(BF16)
    rows_ref[:, :128] = dot(low, rows).astype(BF16)
    rows_ref[:, 128:] = dot(high, rows).astype(BF16)
    for _ in steps:
        pass


def finish(terms, back, dest, scale):
    vmem = pl.BlockSpec(memory_space=pltpu.VMEM)
    return pl.pallas_call(
        functools.partial(finish_kernel, scale),
        out_shape=(jax.ShapeDtypeStruct((864, 8, 128), BF16), jax.ShapeDtypeStruct((ROWS, 256), BF16)),
        in_specs=[vmem] * 3,
        out_specs=(vmem, vmem),
        scratch_shapes=[pltpu.VMEM((BLK, 8, 128), BF16), pltpu.SemaphoreType.DMA((2,))] + reduce_scratch(),
        compiler_params=pltpu.CompilerParams(collective_id=2, has_side_effects=True, vmem_limit_bytes=40 << 20),
    )(terms, back, dest)


def shards(features, dest, placement, weight, grad_out):
    size_x, size_y, size_z, out_channels = grad_out.shape
    own, halo = exchange(dest, features, placement, grad_out.reshape(VOX, out_channels))
    terms, output, back = convolve(own, halo, weight, placement)
    total = ROWS * lax.axis_size("grp") * lax.axis_size("blk")
    weight_grad, grad_rows = finish(terms, back, dest, 1.0 / math.sqrt(total))
    return output.reshape(size_x, size_y, size_z, out_channels), grad_rows, weight_grad.reshape(weight.shape)


def solution(mesh):
    in_specs = (
        P(("grp", "blk"), None),
        P(("grp", "blk"), None),
        P(("grp", "blk"), None),
        P(),
        P("grp", "blk", None, None),
    )
    out_specs = (P("grp", "blk", None, None), P(("grp", "blk"), None), P())
    return jax.shard_map(shards, mesh=mesh, in_specs=in_specs, out_specs=out_specs, check_vma=False)
```

```python
import math

import jax
import jax.numpy as jnp
from jax import lax
from jax.experimental import pallas as pl
from jax.experimental.pallas import tpu as pltpu
from jax.sharding import PartitionSpec as P

MESH = pl.DeviceIdType.MESH
F32, BF16 = jnp.float32, jnp.bfloat16
SIZES = {"x": 4, "y": 8, "z": 8}
PARTS = ((0, 6, "xyz"), (6, 7, "xzy"), (13, 7, "yzx"), (20, 7, "zyx"))
TILE = (8, 128)


VOX, SLOTS, ROWS = 256, 512, 128
GRP, BLK = 8, 64
HALO = 160
BLOCKS = ((0, 4), (4, 4), (8, 4), (12, 4), (16, 1), (17, 1), (18, 1), (19, 1))
SIDES = ((-1, 0), (1, 0), (0, -1), (0, 1), (-1, -1), (-1, 1), (1, -1), (1, 1))


def iota(shape, dim):
    return lax.broadcasted_iota(jnp.int32, shape, dim)


def dot(a, b, dims=((1,), (0,))):
    return lax.dot_general(a, b, (dims, ((), ())), preferred_element_type=F32)


def one(mask):
    return jnp.where(mask, 1.0, 0.0).astype(BF16)


def inner(v):
    return (v & 3) * 64 + (v >> 5) * 8 + ((v >> 2) & 7)


def part_sizes(part):
    first, count, axes = part
    na, nb, nc = (SIZES[a] for a in axes)
    per_core = count * 32 // 2
    n_a = per_core // na
    n_b = -(-n_a // nb)
    return na, nb, nc, per_core, n_a, n_b


def reduce_scratch():
    shapes = []
    for part in PARTS:
        na, nb, nc, per_core, n_a, n_b = part_sizes(part)
        shapes += [
            pltpu.VMEM((na, n_a) + TILE, F32),
            pltpu.VMEM((na - 1, n_a) + TILE, F32),
            pltpu.VMEM((nb * n_b,) + TILE, F32),
            pltpu.VMEM((nb - 1, n_b) + TILE, F32),
            pltpu.VMEM((nc, n_b) + TILE, F32),
            pltpu.VMEM((nb * n_b,) + TILE, BF16),
        ]
        for n in (na, na, nb, nc, nb, na, na):
            shapes += [pltpu.SemaphoreType.DMA((n,)), pltpu.SemaphoreType.DMA((n,))]
    return shapes


PER_PART = 6 + 14


def coords():
    g, b = lax.axis_index("grp"), lax.axis_index("blk")
    return {"x": g // 2, "c": g % 2, "y": b // 8, "z": b % 8}


def device(at, axis, value):
    at = dict(at)
    at[axis] = value
    return (at["x"] * 2 + at["c"], at["y"] * 8 + at["z"])


def row_slots(dest_row, by_row):
    turned = jnp.broadcast_to(dest_row, (ROWS, ROWS))
    wide = turned.astype(F32).T.astype(jnp.int32)
    i, j = iota((ROWS, ROWS), 0), iota((ROWS, ROWS), 1)
    same = wide == turned
    if by_row:
        rank = jnp.sum(jnp.where(same & (j < i), 1.0, 0.0), axis=1, keepdims=True)
        return wide[:, 0:1] * 8 + rank.astype(jnp.int32)
    rank = jnp.sum(jnp.where(same & (i < j), 1.0, 0.0), axis=0, keepdims=True)
    return dest_row * 8 + rank.astype(jnp.int32)


def spread(shape, slot_dim):
    slot, half = iota(shape, slot_dim), iota(shape, 1 - slot_dim)
    return one((half >> 3) * 4 + (half & 3) == slot)


def face_source(row):
    t = row & 31
    far = jnp.where((row & 32) != 0, 7, 0)
    x_side = (t >> 3) * 64 + far * 8 + (t & 7)
    y_side = (t >> 3) * 64 + (t & 7) * 8 + far
    k = (row - 128) >> 3
    corner = (row & 3) * 64 + (k >> 1) * 56 + (k & 1) * 7
    return jnp.where(row < 64, x_side, jnp.where(row < 128, y_side, corner))


def cell_source(row, shift_y):
    z = row // 80
    x = (row >> 3) - z * 10 - 1
    y = (row & 7) + (shift_y - 1)
    in_x, in_y = (x >= 0) & (x < 8), (y >= 0) & (y < 8)
    right, top = jnp.where(x > 7, 1, 0), jnp.where(y > 7, 1, 0)
    inside = z * 64 + x * 8 + y
    x_side = VOX + right * 32 + z * 8 + y
    y_side = VOX + 64 + top * 32 + z * 8 + x
    corner = VOX + 128 + right * 16 + top * 8 + z
    return jnp.where(in_x & in_y, inside, jnp.where(in_y, x_side, jnp.where(in_x, y_side, corner)))


def greet_block(barrier, g, b):
    def signal(r, _):
        pl.semaphore_signal(barrier, inc=1, device_id=(g, (b + r) % BLK), device_id_type=MESH)
        return 0

    lax.fori_loop(1, BLK, signal, 0)


def start_all_to_all(g, b, out_ref, in_ref, sems):
    def send(r, _):
        to = (b + r) % BLK
        pltpu.make_async_remote_copy(
            src_ref=out_ref.at[to],
            dst_ref=in_ref.at[b],
            send_sem=sems.at[0],
            recv_sem=sems.at[1],
            device_id=(g, to),
            device_id_type=MESH,
        ).start()
        return 0

    lax.fori_loop(1, BLK, send, 0)


def end_all_to_all(g, b, out_ref, in_ref, sems):
    pltpu.make_async_remote_copy(
        src_ref=out_ref.at[pl.ds(0, BLK - 1)],
        dst_ref=in_ref.at[pl.ds(0, BLK - 1)],
        send_sem=sems.at[0],
        recv_sem=sems.at[1],
        device_id=(g, (b + 1) % BLK),
        device_id_type=MESH,
    ).wait()


class Reduction:
    def __init__(self, at, scale, terms, result, scratch):
        self.at, self.scale, self.terms, self.result = at, scale, terms, result
        self.sibling = device(at, "c", 1 - at["c"])
        self.sends, self.flights = [], {}
        self.own = [scratch[i * PER_PART : (i + 1) * PER_PART] for i in range(len(PARTS))]

    def copy(self, key, src, dst, sems, r, who):
        made = pltpu.make_async_remote_copy(
            src_ref=src, dst_ref=dst, send_sem=sems[0].at[r], recv_sem=sems[1].at[r], device_id=who, device_id_type=MESH
        )
        made.start()
        self.sends.append(made)
        self.flights[key] = made

    def took(self, *key):
        self.flights[key].wait_recv()

    def parts(self, i):
        first, _, axes = PARTS[i]
        bufs, sems = self.own[i][:6], self.own[i][6:]
        pairs = [sems[k : k + 2] for k in range(0, 14, 2)]
        return axes, part_sizes(PARTS[i]), bufs, pairs

    def chunk(self, i, core, r):
        first, _, axes = PARTS[i]
        na, _, _, per_core, n_a, _ = part_sizes(PARTS[i])
        return pl.ds(first * 32 + core * per_core + (self.at[axes[0]] + r) % na * n_a, n_a)

    def rounds(self, i):
        na = part_sizes(PARTS[i])[0]
        return [*range(1, na), 0]

    def to_core(self, i):
        axes, _, bufs, pairs = self.parts(i)
        for r in self.rounds(i):
            src = self.terms.at[self.chunk(i, 1 - self.at["c"], r)]
            self.copy(("core", i, r), src, bufs[0].at[r], pairs[0], r, self.sibling)

    def to_first(self, i):
        axes, (na, *_), bufs, pairs = self.parts(i)
        for r in self.rounds(i):
            self.took("core", i, r)
            bufs[0][r] = bufs[0][r] + self.terms[self.chunk(i, self.at["c"], r)]
            if r:
                who = device(self.at, axes[0], (self.at[axes[0]] + r) % na)
                self.copy(("a", i, r), bufs[0].at[r], bufs[1].at[r - 1], pairs[1], r, who)

    def to_second(self, i):
        axes, (na, nb, nc, per_core, n_a, n_b), bufs, pairs = self.parts(i)
        total = bufs[0][0]
        for r in range(1, na):
            self.took("a", i, r)
            total = total + bufs[1][r - 1]
        bufs[2][pl.ds(0, n_a)] = total
        if n_a < nb * n_b:
            bufs[2][pl.ds(n_a, nb * n_b - n_a)] = jnp.zeros((nb * n_b - n_a,) + TILE, F32)
        for r in range(1, nb):
            to = (self.at[axes[1]] + r) % nb
            src = bufs[2].at[pl.ds(to * n_b, n_b)]
            self.copy(("b", i, r), src, bufs[3].at[r - 1], pairs[2], r, device(self.at, axes[1], to))

    def to_third(self, i):
        axes, (na, nb, nc, per_core, n_a, n_b), bufs, pairs = self.parts(i)
        total = bufs[2][pl.ds(self.at[axes[1]] * n_b, n_b)]
        for r in range(1, nb):
            self.took("b", i, r)
            total = total + bufs[3][r - 1]
        me = self.at[axes[2]]
        bufs[4][me] = total
        for r in range(1, nc):
            who = device(self.at, axes[2], (me + r) % nc)
            self.copy(("c", i, r), bufs[4].at[me], bufs[4].at[me], pairs[3], r, who)

    def back_second(self, i):
        axes, (na, nb, nc, per_core, n_a, n_b), bufs, pairs = self.parts(i)
        for r in range(1, nc):
            self.took("c", i, r)
        total = bufs[4][0]
        for k in range(1, nc):
            total = total + bufs[4][k]
        me = self.at[axes[1]]
        mine = pl.ds(me * n_b, n_b)
        bufs[5][mine] = (total * self.scale).astype(BF16)
        for r in range(1, nb):
            who = device(self.at, axes[1], (me + r) % nb)
            self.copy(("d", i, r), bufs[5].at[mine], bufs[5].at[mine], pairs[4], r, who)

    def back_first(self, i):
        axes, (na, nb, nc, per_core, n_a, n_b), bufs, pairs = self.parts(i)
        for r in range(1, nb):
            self.took("d", i, r)
        mine = self.chunk(i, self.at["c"], 0)
        whole = bufs[5].at[pl.ds(0, n_a)]
        for r in range(1, na):
            who = device(self.at, axes[0], (self.at[axes[0]] + r) % na)
            self.copy(("e", i, r), whole, self.result.at[mine], pairs[5], r, who)
        self.copy(("f", i, 0), whole, self.result.at[mine], pairs[6], 0, self.sibling)
        self.result[mine] = bufs[5][pl.ds(0, n_a)]

    def back_core(self, i, r):
        axes, (na, *_), bufs, pairs = self.parts(i)
        self.took("e", i, r)
        came = self.result.at[self.chunk(i, self.at["c"], na - r)]
        self.copy(("f", i, r), came, came, pairs[6], r, self.sibling)

    def end(self):
        for i in range(len(PARTS)):
            for r in self.rounds(i):
                self.took("f", i, r)
        for made in self.sends:
            made.wait_send()


def step_kernel(
    scale,
    dest_hbm,
    features_hbm,
    place_hbm,
    grad_hbm,
    weight_hbm,
    result_ref,
    rows_ref,
    output_ref,
    dest_ref,
    features_ref,
    place_ref,
    grad_ref,
    weight_ref,
    terms_ref,
    out,
    came,
    back_out,
    back_came,
    face,
    edge,
    select_ref,
    cells_f,
    cells_g,
    load_sems,
    sems,
    back_sems,
    send_sems,
    recv_sems,
    *scratch,
):
    g, b = lax.axis_index("grp"), lax.axis_index("blk")
    at = coords()
    pairs = (
        (dest_hbm, dest_ref),
        (features_hbm, features_ref),
        (place_hbm, place_ref),
        (grad_hbm, grad_ref),
        (weight_hbm, weight_ref),
    )
    loads = [pltpu.make_async_copy(src, dst, load_sems.at[k]) for k, (src, dst) in enumerate(pairs)]
    for load in loads:
        load.start()
    barrier = pltpu.get_barrier_semaphore()
    greet_block(barrier, g, b)
    for dx in (-1, 1):
        for dy in (-1, 0, 1):
            who = ((g + dx + GRP) % GRP, (b + dy + BLK) % BLK)
            pl.semaphore_signal(barrier, inc=1, device_id=who, device_id_type=MESH)
    for r in range(1, 4):
        who = device(at, "x", (at["x"] + r) % 4)
        pl.semaphore_signal(barrier, inc=1, device_id=who, device_id_type=MESH)

    loads[0].wait()
    slot = row_slots(dest_ref[...], False)
    half = iota((SLOTS, ROWS), 0)
    first, second = half == slot, half == slot + 4
    loads[1].wait()
    packed = dot(one(first), features_ref[:, :128]) + dot(one(second), features_ref[:, 128:])
    held = dot(one(first | second), jnp.ones((ROWS, 128), BF16))
    out[...] = jnp.where(held > 0.5, packed, jnp.inf).reshape(BLK, 8, 128).astype(BF16)
    pl.semaphore_wait(barrier, BLK - 1 + 6 + 3)
    start_all_to_all(g, b, out, came, sems)
    came[b] = out[b]

    loads[2].wait()
    places = jnp.broadcast_to(place_ref[...], (8, VOX)).astype(F32).astype(BF16)
    place8 = dot(places, spread((VOX, SLOTS), 0))[0:1].astype(jnp.int32)
    hits = iota((VOX, SLOTS), 0) == inner(place8)
    low = (iota((VOX, SLOTS), 1) & 4) == 0
    low_hits, high_hits = one(hits & low), one(hits & ~low)
    loads[3].wait()
    grad = dot(one(inner(iota((VOX, VOX), 1)) == iota((VOX, VOX), 0)), grad_ref[...])
    face_of = one(face_source(iota((HALO, VOX), 0)) == iota((HALO, VOX), 1))
    for y in range(3):
        select_ref[y] = one(cell_source(iota((320, 1), 0), y) == iota((320, VOX + HALO), 1))
    for ref in (cells_f, cells_g):
        for y in range(3):
            for z in (0, 5):
                ref[y, z] = jnp.zeros(ref.shape[2:], F32)
    loads[4].wait()

    end_all_to_all(g, b, out, came, sems)
    got = came[...].astype(F32).reshape(SLOTS, 128)
    there = got < jnp.inf
    rows = jnp.where(there, got, 0.0).astype(BF16)
    left = dot(low_hits, rows).astype(BF16)
    right = dot(high_hits, rows).astype(BF16)
    occupied = dot(low_hits, one(there))
    masked = (grad * occupied).astype(BF16)
    cells = jnp.concatenate([left, right, masked], axis=1)
    face[...] = dot(face_of, cells).reshape(HALO // 8, 8, 384).astype(BF16)
    copies = []
    for k, ((place, size), (dx, dy)) in enumerate(zip(BLOCKS, SIDES)):
        opposite = SIDES.index((-dx, -dy))
        made = pltpu.make_async_remote_copy(
            src_ref=face.at[pl.ds(place, size)],
            dst_ref=edge.at[pl.ds(BLOCKS[opposite][0], size)],
            send_sem=send_sems.at[k],
            recv_sem=recv_sems.at[k],
            device_id=((g + dx + GRP) % GRP, (b + dy + BLK) % BLK),
            device_id_type=MESH,
        )
        made.start()
        copies.append(made)
    row = iota((HALO, 1), 0)
    corner = (row - 128) >> 3
    on_x = (row < 64) | (row >= 128)
    on_y = row >= 64
    x_far = jnp.where(row < 64, row >> 5, corner >> 1)
    y_far = jnp.where(row < 128, (row - 64) >> 5, corner & 1)
    at_x = jnp.where(x_far == 1, jnp.where(g == GRP - 1, 1, 0), jnp.where(g == 0, 1, 0))
    at_y = jnp.where(y_far == 1, jnp.where(b == BLK - 1, 1, 0), jnp.where(b == 0, 1, 0))
    beyond = (on_x & (at_x == 1)) | (on_y & (at_y == 1))
    turned = jnp.concatenate([left, right], axis=1).astype(F32).T.astype(BF16)
    for made in copies:
        made.wait()
    halo = jnp.where(beyond, 0.0, edge[...].astype(F32).reshape(HALO, 384)).astype(BF16)
    data = jnp.concatenate([cells, halo], axis=0)

    def shift(ref, part):
        for y in range(3):
            ref[y, 1:5] = dot(select_ref[y], part).reshape(4, 10, 8, part.shape[1])

    def window(ref, x, y, z):
        part = ref[y, z : z + 4, x : x + 8]
        return part.reshape(VOX, part.shape[-1]).astype(BF16)

    def seen(group):
        x, y = group // 3, group % 3
        return jnp.concatenate([window(cells_g, 2 - x, 2 - y, 2 - z) for z in range(3)], axis=1)

    def near(group):
        x, y = group // 3, group % 3
        return jnp.concatenate([window(cells_f, x, y, z) for z in range(3)], axis=1)

    def contribute(groups):
        for group in groups:
            terms = dot(turned, seen(group))
            for z in range(3):
                k = group * 3 + z
                terms_ref[k * 32 : (k + 1) * 32] = terms[:, z * 128 : (z + 1) * 128].reshape(32, 8, 128)

    shift(cells_g, data[:, 256:])
    summed = Reduction(at, scale, terms_ref, result_ref, scratch)
    contribute((4, 5, 6))
    summed.to_core(2)
    contribute((7, 8))
    summed.to_core(3)
    summed.to_first(2)
    contribute((3, 2))
    summed.to_core(1)
    summed.to_first(3)
    contribute((1, 0))
    summed.to_core(0)
    summed.to_first(1)
    summed.to_first(0)

    shift(cells_f, data[:, :256])
    total = jnp.zeros((VOX, 128), F32)
    back = jnp.zeros((VOX, 256), F32)
    for group in range(9):
        weights = [weight_ref[group * 3 + z] for z in range(3)]
        back = back + dot(seen(group), jnp.concatenate(weights, axis=1), ((1,), (1,)))
        total = total + dot(near(group), jnp.concatenate(weights, axis=0))
    natural = one(inner(iota((VOX, VOX), 0)) == iota((VOX, VOX), 1))
    output_ref[...] = dot(natural, (total * occupied).astype(BF16)).astype(BF16)
    grid_l = (back[:, :128] * occupied).astype(BF16)
    grid_r = (back[:, 128:] * occupied).astype(BF16)
    returned = dot(low_hits, grid_l, ((0,), (0,))) + dot(high_hits, grid_r, ((0,), (0,)))
    back_out[...] = returned.reshape(BLK, 8, 128).astype(BF16)

    order = (0, 1, 2, 3)
    for i in order:
        summed.to_second(i)
    start_all_to_all(g, b, back_out, back_came, back_sems)
    back_came[b] = back_out[b]
    for i in order:
        summed.to_third(i)
    for i in order:
        summed.back_second(i)
    for i in order:
        summed.back_first(i)
    for r in range(1, 8):
        for i in order:
            if r < part_sizes(PARTS[i])[0]:
                summed.back_core(i, r)
    end_all_to_all(g, b, back_out, back_came, back_sems)
    slot = row_slots(dest_ref[...], True)
    half = iota((ROWS, SLOTS), 1)
    rows = back_came[...].astype(F32).reshape(SLOTS, 128).astype(BF16)
    rows_ref[:, :128] = dot(one(half == slot), rows).astype(BF16)
    rows_ref[:, 128:] = dot(one(half == slot + 4), rows).astype(BF16)
    summed.end()


def shards(features, dest, placement, weight, grad_out):
    count = ROWS * lax.axis_size("grp") * lax.axis_size("blk")
    vmem, hbm = pl.BlockSpec(memory_space=pltpu.VMEM), pl.BlockSpec(memory_space=pltpu.HBM)
    tiles = pltpu.VMEM((BLK, 8, 128), BF16)
    weight_grad, grad_rows, output = pl.pallas_call(
        lambda *refs: step_kernel(1.0 / math.sqrt(count), *refs),
        out_shape=(
            jax.ShapeDtypeStruct((864, 8, 128), BF16),
            jax.ShapeDtypeStruct((ROWS, 256), BF16),
            jax.ShapeDtypeStruct((VOX, 128), BF16),
        ),
        in_specs=[hbm] * 5,
        out_specs=(vmem,) * 3,
        scratch_shapes=[
            pltpu.VMEM((1, ROWS), jnp.int32),
            pltpu.VMEM((ROWS, 256), BF16),
            pltpu.VMEM((1, VOX), jnp.int32),
            pltpu.VMEM((VOX, 128), BF16),
            pltpu.VMEM((27, 256, 128), BF16),
            pltpu.VMEM((864, 8, 128), F32),
            tiles,
            tiles,
            tiles,
            tiles,
            pltpu.VMEM((HALO // 8, 8, 384), BF16),
            pltpu.VMEM((HALO // 8, 8, 384), BF16),
            pltpu.VMEM((3, 320, VOX + HALO), BF16),
            pltpu.VMEM((3, 6, 10, 8, 256), F32),
            pltpu.VMEM((3, 6, 10, 8, 128), F32),
            pltpu.SemaphoreType.DMA((5,)),
            pltpu.SemaphoreType.DMA((2,)),
            pltpu.SemaphoreType.DMA((2,)),
            pltpu.SemaphoreType.DMA((8,)),
            pltpu.SemaphoreType.DMA((8,)),
        ]
        + reduce_scratch(),
        name="step",
        compiler_params=pltpu.CompilerParams(collective_id=1, has_side_effects=True, vmem_limit_bytes=48 << 20),
    )(dest.reshape(1, ROWS), features, placement, grad_out.reshape(VOX, 128), weight)
    return output.reshape(grad_out.shape), grad_rows, weight_grad.reshape(weight.shape)


def solution(mesh):
    in_specs = (
        P(("grp", "blk"), None),
        P(("grp", "blk"), None),
        P(("grp", "blk"), None),
        P(),
        P("grp", "blk", None, None),
    )
    out_specs = (P("grp", "blk", None, None), P(("grp", "blk"), None), P())
    return jax.shard_map(shards, mesh=mesh, in_specs=in_specs, out_specs=out_specs, check_vma=False)
```

```python
import math

import jax
import jax.numpy as jnp
from jax import lax
from jax.experimental import pallas as pl
from jax.experimental.pallas import tpu as pltpu
from jax.sharding import PartitionSpec as P

MESH = pl.DeviceIdType.MESH
F32, BF16 = jnp.float32, jnp.bfloat16
SIZES = {"x": 4, "y": 8, "z": 8}
PARTS = ((0, 6, "xyz"), (6, 7, "xzy"), (13, 7, "yzx"), (20, 7, "zyx"))
TILE = (8, 128)


VOX, SLOTS, ROWS = 256, 512, 128
GRP, BLK = 8, 64
HALO = 160
BLOCKS = ((0, 4), (4, 4), (8, 4), (12, 4), (16, 1), (17, 1), (18, 1), (19, 1))
SIDES = ((-1, 0), (1, 0), (0, -1), (0, 1), (-1, -1), (-1, 1), (1, -1), (1, 1))


def iota(shape, dim):
    return lax.broadcasted_iota(jnp.int32, shape, dim)


def dot(a, b, dims=((1,), (0,))):
    return lax.dot_general(a, b, (dims, ((), ())), preferred_element_type=F32)


def one(mask):
    return jnp.where(mask, 1.0, 0.0).astype(BF16)


def inner(v):
    return (v & 3) * 64 + (v >> 5) * 8 + ((v >> 2) & 7)


def part_sizes(part):
    first, count, axes = part
    na, nb, nc = (SIZES[a] for a in axes)
    per_core = count * 32 // 2
    n_a = per_core // na
    n_b = -(-n_a // nb)
    return na, nb, nc, per_core, n_a, n_b


def reduce_scratch():
    shapes = []
    for part in PARTS:
        na, nb, nc, per_core, n_a, n_b = part_sizes(part)
        shapes += [
            pltpu.VMEM((na, n_a) + TILE, F32),
            pltpu.VMEM((na - 1, n_a) + TILE, F32),
            pltpu.VMEM((nb * n_b,) + TILE, F32),
            pltpu.VMEM((nb - 1, n_b) + TILE, F32),
            pltpu.VMEM((nc, n_b) + TILE, F32),
            pltpu.VMEM((nb * n_b,) + TILE, BF16),
        ]
        for n in (na, na, nb, nc, nb, na, na):
            shapes += [pltpu.SemaphoreType.DMA((n,)), pltpu.SemaphoreType.DMA((n,))]
    return shapes


PER_PART = 6 + 14


def coords():
    g, b = lax.axis_index("grp"), lax.axis_index("blk")
    return {"x": g // 2, "c": g % 2, "y": b // 8, "z": b % 8}


def device(at, axis, value):
    at = dict(at)
    at[axis] = value
    return (at["x"] * 2 + at["c"], at["y"] * 8 + at["z"])


def row_slots(dest_row, by_row):
    turned = jnp.broadcast_to(dest_row, (ROWS, ROWS))
    wide = turned.astype(F32).T.astype(jnp.int32)
    i, j = iota((ROWS, ROWS), 0), iota((ROWS, ROWS), 1)
    same = wide == turned
    if by_row:
        rank = jnp.sum(jnp.where(same & (j < i), 1.0, 0.0), axis=1, keepdims=True)
        return wide[:, 0:1] * 8 + rank.astype(jnp.int32)
    rank = jnp.sum(jnp.where(same & (i < j), 1.0, 0.0), axis=0, keepdims=True)
    return dest_row * 8 + rank.astype(jnp.int32)


def spread(shape, slot_dim):
    slot, half = iota(shape, slot_dim), iota(shape, 1 - slot_dim)
    return one((half >> 3) * 4 + (half & 3) == slot)


def face_source(row):
    t = row & 31
    far = jnp.where((row & 32) != 0, 7, 0)
    x_side = (t >> 3) * 64 + far * 8 + (t & 7)
    y_side = (t >> 3) * 64 + (t & 7) * 8 + far
    k = (row - 128) >> 3
    corner = (row & 3) * 64 + (k >> 1) * 56 + (k & 1) * 7
    return jnp.where(row < 64, x_side, jnp.where(row < 128, y_side, corner))


def cell_source(row, shift_y):
    z = row // 80
    x = (row >> 3) - z * 10 - 1
    y = (row & 7) + (shift_y - 1)
    in_x, in_y = (x >= 0) & (x < 8), (y >= 0) & (y < 8)
    right, top = jnp.where(x > 7, 1, 0), jnp.where(y > 7, 1, 0)
    inside = z * 64 + x * 8 + y
    x_side = VOX + right * 32 + z * 8 + y
    y_side = VOX + 64 + top * 32 + z * 8 + x
    corner = VOX + 128 + right * 16 + top * 8 + z
    return jnp.where(in_x & in_y, inside, jnp.where(in_y, x_side, jnp.where(in_x, y_side, corner)))


def greet_block(barrier, g, b):
    def signal(r, _):
        pl.semaphore_signal(barrier, inc=1, device_id=(g, (b + r) % BLK), device_id_type=MESH)
        return 0

    lax.fori_loop(1, BLK, signal, 0)


def start_all_to_all(g, b, out_ref, in_ref, sems):
    def send(r, _):
        to = (b + r) % BLK
        pltpu.make_async_remote_copy(
            src_ref=out_ref.at[to],
            dst_ref=in_ref.at[b],
            send_sem=sems.at[0],
            recv_sem=sems.at[1],
            device_id=(g, to),
            device_id_type=MESH,
        ).start()
        return 0

    lax.fori_loop(1, BLK, send, 0)


def end_all_to_all(g, b, out_ref, in_ref, sems):
    pltpu.make_async_remote_copy(
        src_ref=out_ref.at[pl.ds(0, BLK - 1)],
        dst_ref=in_ref.at[pl.ds(0, BLK - 1)],
        send_sem=sems.at[0],
        recv_sem=sems.at[1],
        device_id=(g, (b + 1) % BLK),
        device_id_type=MESH,
    ).wait()


class Reduction:
    def __init__(self, at, scale, terms, result, scratch):
        self.at, self.scale, self.terms, self.result = at, scale, terms, result
        self.sibling = device(at, "c", 1 - at["c"])
        self.sends, self.flights = [], {}
        self.own = [scratch[i * PER_PART : (i + 1) * PER_PART] for i in range(len(PARTS))]

    def copy(self, key, src, dst, sems, r, who):
        made = pltpu.make_async_remote_copy(
            src_ref=src, dst_ref=dst, send_sem=sems[0].at[r], recv_sem=sems[1].at[r], device_id=who, device_id_type=MESH
        )
        made.start()
        self.sends.append(made)
        self.flights[key] = made

    def took(self, *key):
        self.flights[key].wait_recv()

    def parts(self, i):
        first, _, axes = PARTS[i]
        bufs, sems = self.own[i][:6], self.own[i][6:]
        pairs = [sems[k : k + 2] for k in range(0, 14, 2)]
        return axes, part_sizes(PARTS[i]), bufs, pairs

    def chunk(self, i, core, r):
        first, _, axes = PARTS[i]
        na, _, _, per_core, n_a, _ = part_sizes(PARTS[i])
        return pl.ds(first * 32 + core * per_core + (self.at[axes[0]] + r) % na * n_a, n_a)

    def rounds(self, i):
        na = part_sizes(PARTS[i])[0]
        return [*range(1, na), 0]

    def to_core(self, i):
        axes, _, bufs, pairs = self.parts(i)
        for r in self.rounds(i):
            src = self.terms.at[self.chunk(i, 1 - self.at["c"], r)]
            self.copy(("core", i, r), src, bufs[0].at[r], pairs[0], r, self.sibling)

    def to_first(self, i):
        axes, (na, *_), bufs, pairs = self.parts(i)
        for r in self.rounds(i):
            self.took("core", i, r)
            bufs[0][r] = bufs[0][r] + self.terms[self.chunk(i, self.at["c"], r)]
            if r:
                who = device(self.at, axes[0], (self.at[axes[0]] + r) % na)
                self.copy(("a", i, r), bufs[0].at[r], bufs[1].at[r - 1], pairs[1], r, who)

    def to_second(self, i):
        axes, (na, nb, nc, per_core, n_a, n_b), bufs, pairs = self.parts(i)
        total = bufs[0][0]
        for r in range(1, na):
            self.took("a", i, r)
            total = total + bufs[1][r - 1]
        bufs[2][pl.ds(0, n_a)] = total
        if n_a < nb * n_b:
            bufs[2][pl.ds(n_a, nb * n_b - n_a)] = jnp.zeros((nb * n_b - n_a,) + TILE, F32)
        for r in range(1, nb):
            to = (self.at[axes[1]] + r) % nb
            src = bufs[2].at[pl.ds(to * n_b, n_b)]
            self.copy(("b", i, r), src, bufs[3].at[r - 1], pairs[2], r, device(self.at, axes[1], to))

    def to_third(self, i):
        axes, (na, nb, nc, per_core, n_a, n_b), bufs, pairs = self.parts(i)
        total = bufs[2][pl.ds(self.at[axes[1]] * n_b, n_b)]
        for r in range(1, nb):
            self.took("b", i, r)
            total = total + bufs[3][r - 1]
        me = self.at[axes[2]]
        bufs[4][me] = total
        for r in range(1, nc):
            who = device(self.at, axes[2], (me + r) % nc)
            self.copy(("c", i, r), bufs[4].at[me], bufs[4].at[me], pairs[3], r, who)

    def back_second(self, i):
        axes, (na, nb, nc, per_core, n_a, n_b), bufs, pairs = self.parts(i)
        for r in range(1, nc):
            self.took("c", i, r)
        total = bufs[4][0]
        for k in range(1, nc):
            total = total + bufs[4][k]
        me = self.at[axes[1]]
        mine = pl.ds(me * n_b, n_b)
        bufs[5][mine] = (total * self.scale).astype(BF16)
        for r in range(1, nb):
            who = device(self.at, axes[1], (me + r) % nb)
            self.copy(("d", i, r), bufs[5].at[mine], bufs[5].at[mine], pairs[4], r, who)

    def back_first(self, i):
        axes, (na, nb, nc, per_core, n_a, n_b), bufs, pairs = self.parts(i)
        for r in range(1, nb):
            self.took("d", i, r)
        mine = self.chunk(i, self.at["c"], 0)
        whole = bufs[5].at[pl.ds(0, n_a)]
        for r in range(1, na):
            who = device(self.at, axes[0], (self.at[axes[0]] + r) % na)
            self.copy(("e", i, r), whole, self.result.at[mine], pairs[5], r, who)
        self.copy(("f", i, 0), whole, self.result.at[mine], pairs[6], 0, self.sibling)
        self.result[mine] = bufs[5][pl.ds(0, n_a)]

    def back_core(self, i, r):
        axes, (na, *_), bufs, pairs = self.parts(i)
        self.took("e", i, r)
        came = self.result.at[self.chunk(i, self.at["c"], na - r)]
        self.copy(("f", i, r), came, came, pairs[6], r, self.sibling)

    def end(self):
        for i in range(len(PARTS)):
            for r in self.rounds(i):
                self.took("f", i, r)
        for made in self.sends:
            made.wait_send()


def step_kernel(
    scale,
    dest_hbm,
    features_hbm,
    place_hbm,
    grad_hbm,
    weight_hbm,
    result_ref,
    rows_ref,
    output_ref,
    dest_ref,
    features_ref,
    place_ref,
    grad_ref,
    weight_ref,
    terms_ref,
    out,
    came,
    back_out,
    back_came,
    face,
    edge,
    select_ref,
    take_ref,
    cells_f,
    cells_g,
    load_sems,
    sems,
    back_sems,
    send_sems,
    recv_sems,
    *scratch,
):
    g, b = lax.axis_index("grp"), lax.axis_index("blk")
    at = coords()
    pairs = (
        (dest_hbm, dest_ref),
        (features_hbm, features_ref),
        (place_hbm, place_ref),
        (grad_hbm, grad_ref),
        (weight_hbm, weight_ref),
    )
    loads = [pltpu.make_async_copy(src, dst, load_sems.at[k]) for k, (src, dst) in enumerate(pairs)]
    for load in loads:
        load.start()
    barrier = pltpu.get_barrier_semaphore()
    greet_block(barrier, g, b)
    for dx in (-1, 1):
        for dy in (-1, 0, 1):
            who = ((g + dx + GRP) % GRP, (b + dy + BLK) % BLK)
            pl.semaphore_signal(barrier, inc=1, device_id=who, device_id_type=MESH)
    for r in range(1, 4):
        who = device(at, "x", (at["x"] + r) % 4)
        pl.semaphore_signal(barrier, inc=1, device_id=who, device_id_type=MESH)

    loads[0].wait()
    slot = row_slots(dest_ref[...], False)
    half = iota((SLOTS, ROWS), 0)
    first, second = half == slot, half == slot + 4
    loads[1].wait()
    packed = dot(one(first), features_ref[:, :128]) + dot(one(second), features_ref[:, 128:])
    held = dot(one(first | second), jnp.ones((ROWS, 128), BF16))
    out[...] = jnp.where(held > 0.5, packed, jnp.inf).reshape(BLK, 8, 128).astype(BF16)
    pl.semaphore_wait(barrier, BLK - 1 + 6 + 3)
    start_all_to_all(g, b, out, came, sems)
    came[b] = out[b]

    loads[2].wait()
    places = jnp.broadcast_to(place_ref[...], (8, VOX)).astype(F32).astype(BF16)
    place8 = dot(places, spread((VOX, SLOTS), 0))[0:1].astype(jnp.int32)
    hits = iota((VOX, SLOTS), 0) == inner(place8)
    low = (iota((VOX, SLOTS), 1) & 4) == 0
    low_hits, high_hits = one(hits & low), one(hits & ~low)
    loads[3].wait()
    grad = dot(one(inner(iota((VOX, VOX), 1)) == iota((VOX, VOX), 0)), grad_ref[...])
    face_of = one(face_source(iota((HALO, VOX), 0)) == iota((HALO, VOX), 1))
    for y in range(3):
        select_ref[y] = one(cell_source(iota((320, 1), 0), y) == iota((320, VOX + HALO), 1))
    back_slot, half = row_slots(dest_ref[...], True), iota((ROWS, SLOTS), 1)
    take_ref[0] = one(half == back_slot)
    take_ref[1] = one(half == back_slot + 4)
    for ref in (cells_f, cells_g):
        for y in range(3):
            for z in (0, 5):
                ref[y, z] = jnp.zeros(ref.shape[2:], F32)
    loads[4].wait()

    end_all_to_all(g, b, out, came, sems)
    got = came[...].astype(F32).reshape(SLOTS, 128)
    there = got < jnp.inf
    rows = jnp.where(there, got, 0.0).astype(BF16)
    left = dot(low_hits, rows).astype(BF16)
    right = dot(high_hits, rows).astype(BF16)
    occupied = dot(low_hits, one(there))
    masked = (grad * occupied).astype(BF16)
    cells = jnp.concatenate([left, right, masked], axis=1)
    face[...] = dot(face_of, cells).reshape(HALO // 8, 8, 384).astype(BF16)
    copies = []
    for k, ((place, size), (dx, dy)) in enumerate(zip(BLOCKS, SIDES)):
        opposite = SIDES.index((-dx, -dy))
        made = pltpu.make_async_remote_copy(
            src_ref=face.at[pl.ds(place, size)],
            dst_ref=edge.at[pl.ds(BLOCKS[opposite][0], size)],
            send_sem=send_sems.at[k],
            recv_sem=recv_sems.at[k],
            device_id=((g + dx + GRP) % GRP, (b + dy + BLK) % BLK),
            device_id_type=MESH,
        )
        made.start()
        copies.append(made)
    row = iota((HALO, 1), 0)
    corner = (row - 128) >> 3
    on_x = (row < 64) | (row >= 128)
    on_y = row >= 64
    x_far = jnp.where(row < 64, row >> 5, corner >> 1)
    y_far = jnp.where(row < 128, (row - 64) >> 5, corner & 1)
    at_x = jnp.where(x_far == 1, jnp.where(g == GRP - 1, 1, 0), jnp.where(g == 0, 1, 0))
    at_y = jnp.where(y_far == 1, jnp.where(b == BLK - 1, 1, 0), jnp.where(b == 0, 1, 0))
    beyond = (on_x & (at_x == 1)) | (on_y & (at_y == 1))
    turned = jnp.concatenate([left, right], axis=1).astype(F32).T.astype(BF16)
    for made in copies:
        made.wait()
    halo = jnp.where(beyond, 0.0, edge[...].astype(F32).reshape(HALO, 384)).astype(BF16)
    data = jnp.concatenate([cells, halo], axis=0)

    def shift(ref, part):
        for y in range(3):
            ref[y, 1:5] = dot(select_ref[y], part).reshape(4, 10, 8, part.shape[1])

    def window(ref, x, y, z):
        part = ref[y, z : z + 4, x : x + 8]
        return part.reshape(VOX, part.shape[-1]).astype(BF16)

    def seen(group):
        x, y = group // 3, group % 3
        return jnp.concatenate([window(cells_g, 2 - x, 2 - y, 2 - z) for z in range(3)], axis=1)

    def near(group):
        x, y = group // 3, group % 3
        return jnp.concatenate([window(cells_f, x, y, z) for z in range(3)], axis=1)

    def contribute(groups):
        for group in groups:
            terms = dot(turned, seen(group))
            for z in range(3):
                k = group * 3 + z
                terms_ref[k * 32 : (k + 1) * 32] = terms[:, z * 128 : (z + 1) * 128].reshape(32, 8, 128)

    shift(cells_g, data[:, 256:])
    summed = Reduction(at, scale, terms_ref, result_ref, scratch)
    contribute((4, 5, 6))
    summed.to_core(2)
    contribute((7, 8))
    summed.to_core(3)
    summed.to_first(2)
    contribute((3, 2))
    summed.to_core(1)
    summed.to_first(3)
    contribute((1, 0))
    summed.to_core(0)
    summed.to_first(1)
    summed.to_first(0)

    shift(cells_f, data[:, :256])
    total = jnp.zeros((VOX, 128), F32)
    back = jnp.zeros((VOX, 256), F32)
    for group in range(9):
        weights = [weight_ref[group * 3 + z] for z in range(3)]
        back = back + dot(seen(group), jnp.concatenate(weights, axis=1), ((1,), (1,)))
        total = total + dot(near(group), jnp.concatenate(weights, axis=0))
    natural = one(inner(iota((VOX, VOX), 0)) == iota((VOX, VOX), 1))
    output_ref[...] = dot(natural, (total * occupied).astype(BF16)).astype(BF16)
    grid_l = (back[:, :128] * occupied).astype(BF16)
    grid_r = (back[:, 128:] * occupied).astype(BF16)
    returned = dot(low_hits, grid_l, ((0,), (0,))) + dot(high_hits, grid_r, ((0,), (0,)))
    back_out[...] = returned.reshape(BLK, 8, 128).astype(BF16)

    order = (1, 2, 3, 0)
    for i in order:
        summed.to_second(i)
    for i in order:
        summed.to_third(i)
    start_all_to_all(g, b, back_out, back_came, back_sems)
    back_came[b] = back_out[b]
    for i in order:
        summed.back_second(i)
    for i in order:
        summed.back_first(i)
    end_all_to_all(g, b, back_out, back_came, back_sems)
    rows = back_came[...].astype(F32).reshape(SLOTS, 128).astype(BF16)
    rows_ref[:, :128] = dot(take_ref[0], rows).astype(BF16)
    rows_ref[:, 128:] = dot(take_ref[1], rows).astype(BF16)
    for r in range(1, 8):
        for i in order:
            if r < part_sizes(PARTS[i])[0]:
                summed.back_core(i, r)
    summed.end()


def store_kernel(*refs):
    count = len(refs) // 2
    sems = refs[-1]
    copies = [pltpu.make_async_copy(refs[k], refs[count + k], sems.at[k]) for k in range(count)]
    for made in copies:
        made.start()
    for made in copies:
        made.wait()


def store(arrays):
    vmem, hbm = pl.BlockSpec(memory_space=pltpu.VMEM), pl.BlockSpec(memory_space=pltpu.HBM)
    return pl.pallas_call(
        store_kernel,
        out_shape=[jax.ShapeDtypeStruct(a.shape, a.dtype) for a in arrays],
        in_specs=[vmem] * len(arrays),
        out_specs=[hbm] * len(arrays),
        scratch_shapes=[pltpu.SemaphoreType.DMA((len(arrays),))],
        name="store",
        compiler_params=pltpu.CompilerParams(vmem_limit_bytes=8 << 20),
    )(*arrays)


def shards(features, dest, placement, weight, grad_out):
    count = ROWS * lax.axis_size("grp") * lax.axis_size("blk")
    vmem, hbm = pl.BlockSpec(memory_space=pltpu.VMEM), pl.BlockSpec(memory_space=pltpu.HBM)
    tiles = pltpu.VMEM((BLK, 8, 128), BF16)
    inputs = (dest.reshape(1, ROWS), features, placement, grad_out.reshape(VOX, 128), weight)
    weight_grad, grad_rows, output = pl.pallas_call(
        lambda *refs: step_kernel(1.0 / math.sqrt(count), *refs),
        out_shape=(
            jax.ShapeDtypeStruct((864, 8, 128), BF16),
            jax.ShapeDtypeStruct((ROWS, 256), BF16),
            jax.ShapeDtypeStruct((VOX, 128), BF16),
        ),
        in_specs=[hbm] * 5,
        out_specs=(vmem,) * 3,
        scratch_shapes=[
            pltpu.VMEM((1, ROWS), jnp.int32),
            pltpu.VMEM((ROWS, 256), BF16),
            pltpu.VMEM((1, VOX), jnp.int32),
            pltpu.VMEM((VOX, 128), BF16),
            pltpu.VMEM((27, 256, 128), BF16),
            pltpu.VMEM((864, 8, 128), F32),
            tiles,
            tiles,
            tiles,
            tiles,
            pltpu.VMEM((HALO // 8, 8, 384), BF16),
            pltpu.VMEM((HALO // 8, 8, 384), BF16),
            pltpu.VMEM((3, 320, VOX + HALO), BF16),
            pltpu.VMEM((2, ROWS, SLOTS), BF16),
            pltpu.VMEM((3, 6, 10, 8, 256), F32),
            pltpu.VMEM((3, 6, 10, 8, 128), F32),
            pltpu.SemaphoreType.DMA((5,)),
            pltpu.SemaphoreType.DMA((2,)),
            pltpu.SemaphoreType.DMA((2,)),
            pltpu.SemaphoreType.DMA((8,)),
            pltpu.SemaphoreType.DMA((8,)),
        ]
        + reduce_scratch(),
        name="step",
        compiler_params=pltpu.CompilerParams(collective_id=1, has_side_effects=True, vmem_limit_bytes=54_000_000),
    )(*(pltpu.with_memory_space_constraint(a, pltpu.HBM) for a in inputs))
    weight_grad, grad_rows, output = store((weight_grad, grad_rows, output))
    return output.reshape(grad_out.shape), grad_rows, weight_grad.reshape(weight.shape)


def solution(mesh):
    in_specs = (
        P(("grp", "blk"), None),
        P(("grp", "blk"), None),
        P(("grp", "blk"), None),
        P(),
        P("grp", "blk", None, None),
    )
    out_specs = (P("grp", "blk", None, None), P(("grp", "blk"), None), P())
    return jax.shard_map(shards, mesh=mesh, in_specs=in_specs, out_specs=out_specs, check_vma=False)
```

```python
import math

import jax
import jax.numpy as jnp
from jax import lax
from jax.experimental import pallas as pl
from jax.experimental.pallas import tpu as pltpu
from jax.sharding import PartitionSpec as P

MESH = pl.DeviceIdType.MESH
F32, BF16 = jnp.float32, jnp.bfloat16
SIZES = {"x": 4, "y": 8, "z": 8}
PARTS = ((0, 6, "xyz"), (6, 7, "xzy"), (13, 7, "yzx"), (20, 7, "zyx"))
TILE = (8, 128)


VOX, SLOTS, ROWS = 256, 512, 128
GRP, BLK = 8, 64
HALO = 160
BLOCKS = ((0, 4), (4, 4), (8, 4), (12, 4), (16, 1), (17, 1), (18, 1), (19, 1))
SIDES = ((-1, 0), (1, 0), (0, -1), (0, 1), (-1, -1), (-1, 1), (1, -1), (1, 1))


def iota(shape, dim):
    return lax.broadcasted_iota(jnp.int32, shape, dim)


def dot(a, b, dims=((1,), (0,))):
    return lax.dot_general(a, b, (dims, ((), ())), preferred_element_type=F32)


def one(mask):
    return jnp.where(mask, 1.0, 0.0).astype(BF16)


def inner(v):
    return (v & 3) * 64 + (v >> 5) * 8 + ((v >> 2) & 7)


def part_sizes(part):
    first, count, axes = part
    na, nb, nc = (SIZES[a] for a in axes)
    per_core = count * 32 // 2
    n_a = per_core // na
    n_b = -(-n_a // nb)
    return na, nb, nc, per_core, n_a, n_b


def reduce_scratch():
    shapes = []
    for part in PARTS:
        na, nb, nc, per_core, n_a, n_b = part_sizes(part)
        shapes += [
            pltpu.VMEM((na, n_a) + TILE, F32),
            pltpu.VMEM((na - 1, n_a) + TILE, F32),
            pltpu.VMEM((nb * n_b,) + TILE, F32),
            pltpu.VMEM((nb - 1, n_b) + TILE, F32),
            pltpu.VMEM((nc, n_b) + TILE, F32),
            pltpu.VMEM((nb * n_b,) + TILE, BF16),
        ]
        for n in (na, na, nb, nc, nb, na, na):
            shapes += [pltpu.SemaphoreType.DMA((n,)), pltpu.SemaphoreType.DMA((n,))]
    return shapes


PER_PART = 6 + 14


def coords():
    g, b = lax.axis_index("grp"), lax.axis_index("blk")
    return {"x": g // 2, "c": g % 2, "y": b // 8, "z": b % 8}


def device(at, axis, value):
    at = dict(at)
    at[axis] = value
    return (at["x"] * 2 + at["c"], at["y"] * 8 + at["z"])


def row_slots(dest_row, by_row):
    turned = jnp.broadcast_to(dest_row, (ROWS, ROWS))
    wide = turned.astype(F32).T.astype(jnp.int32)
    i, j = iota((ROWS, ROWS), 0), iota((ROWS, ROWS), 1)
    same = wide == turned
    if by_row:
        rank = jnp.sum(jnp.where(same & (j < i), 1.0, 0.0), axis=1, keepdims=True)
        return wide[:, 0:1] * 8 + rank.astype(jnp.int32)
    rank = jnp.sum(jnp.where(same & (i < j), 1.0, 0.0), axis=0, keepdims=True)
    return dest_row * 8 + rank.astype(jnp.int32)


def spread(shape, slot_dim):
    slot, half = iota(shape, slot_dim), iota(shape, 1 - slot_dim)
    return one((half >> 3) * 4 + (half & 3) == slot)


def face_source(row):
    t = row & 31
    far = jnp.where((row & 32) != 0, 7, 0)
    x_side = (t >> 3) * 64 + far * 8 + (t & 7)
    y_side = (t >> 3) * 64 + (t & 7) * 8 + far
    k = (row - 128) >> 3
    corner = (row & 3) * 64 + (k >> 1) * 56 + (k & 1) * 7
    return jnp.where(row < 64, x_side, jnp.where(row < 128, y_side, corner))


def cell_source(row, shift_y):
    z = row // 80
    x = (row >> 3) - z * 10 - 1
    y = (row & 7) + (shift_y - 1)
    in_x, in_y = (x >= 0) & (x < 8), (y >= 0) & (y < 8)
    right, top = jnp.where(x > 7, 1, 0), jnp.where(y > 7, 1, 0)
    inside = z * 64 + x * 8 + y
    x_side = VOX + right * 32 + z * 8 + y
    y_side = VOX + 64 + top * 32 + z * 8 + x
    corner = VOX + 128 + right * 16 + top * 8 + z
    return jnp.where(in_x & in_y, inside, jnp.where(in_y, x_side, jnp.where(in_x, y_side, corner)))


def greet_block(barrier, g, b):
    def signal(r, _):
        pl.semaphore_signal(barrier, inc=1, device_id=(g, (b + r) % BLK), device_id_type=MESH)
        return 0

    lax.fori_loop(1, BLK, signal, 0)


def far_first(i):
    return 4 + i // 2 - i % 2 * (i // 2 * 2 + 1)


def start_all_to_all(g, b, out_ref, in_ref, sems):
    def send(i, _):
        to = (b // 8 + far_first(i // 8)) % 8 * 8 + (b % 8 + far_first(i % 8)) % 8
        pltpu.make_async_remote_copy(
            src_ref=out_ref.at[to],
            dst_ref=in_ref.at[b],
            send_sem=sems.at[0],
            recv_sem=sems.at[1],
            device_id=(g, to),
            device_id_type=MESH,
        ).start()
        return 0

    lax.fori_loop(0, BLK - 1, send, 0)


def end_all_to_all(g, b, out_ref, in_ref, sems):
    pltpu.make_async_remote_copy(
        src_ref=out_ref.at[pl.ds(0, BLK - 1)],
        dst_ref=in_ref.at[pl.ds(0, BLK - 1)],
        send_sem=sems.at[0],
        recv_sem=sems.at[1],
        device_id=(g, (b + 1) % BLK),
        device_id_type=MESH,
    ).wait()


def away(n):
    return sorted(range(1, n), key=lambda r: (-min(r, n - r), r))


class Reduction:
    def __init__(self, at, scale, terms, result, scratch):
        self.at, self.scale, self.terms, self.result = at, scale, terms, result
        self.sibling = device(at, "c", 1 - at["c"])
        self.sends, self.flights = [], {}
        self.own = [scratch[i * PER_PART : (i + 1) * PER_PART] for i in range(len(PARTS))]

    def copy(self, key, src, dst, sems, r, who):
        made = pltpu.make_async_remote_copy(
            src_ref=src, dst_ref=dst, send_sem=sems[0].at[r], recv_sem=sems[1].at[r], device_id=who, device_id_type=MESH
        )
        made.start()
        self.sends.append(made)
        self.flights[key] = made

    def took(self, *key):
        self.flights[key].wait_recv()

    def parts(self, i):
        first, _, axes = PARTS[i]
        bufs, sems = self.own[i][:6], self.own[i][6:]
        pairs = [sems[k : k + 2] for k in range(0, 14, 2)]
        return axes, part_sizes(PARTS[i]), bufs, pairs

    def chunk(self, i, core, r):
        first, _, axes = PARTS[i]
        na, _, _, per_core, n_a, _ = part_sizes(PARTS[i])
        return pl.ds(first * 32 + core * per_core + (self.at[axes[0]] + r) % na * n_a, n_a)

    def rounds(self, i):
        return [*away(part_sizes(PARTS[i])[0]), 0]

    def to_core(self, i):
        axes, _, bufs, pairs = self.parts(i)
        for r in self.rounds(i):
            src = self.terms.at[self.chunk(i, 1 - self.at["c"], r)]
            self.copy(("core", i, r), src, bufs[0].at[r], pairs[0], r, self.sibling)

    def to_first(self, i):
        axes, (na, *_), bufs, pairs = self.parts(i)
        for r in self.rounds(i):
            self.took("core", i, r)
            bufs[0][r] = bufs[0][r] + self.terms[self.chunk(i, self.at["c"], r)]
            if r:
                who = device(self.at, axes[0], (self.at[axes[0]] + r) % na)
                self.copy(("a", i, r), bufs[0].at[r], bufs[1].at[r - 1], pairs[1], r, who)

    def to_second(self, i):
        axes, (na, nb, nc, per_core, n_a, n_b), bufs, pairs = self.parts(i)
        total = bufs[0][0]
        for r in range(1, na):
            self.took("a", i, r)
            total = total + bufs[1][r - 1]
        bufs[2][pl.ds(0, n_a)] = total
        if n_a < nb * n_b:
            bufs[2][pl.ds(n_a, nb * n_b - n_a)] = jnp.zeros((nb * n_b - n_a,) + TILE, F32)
        for r in away(nb):
            to = (self.at[axes[1]] + r) % nb
            src = bufs[2].at[pl.ds(to * n_b, n_b)]
            self.copy(("b", i, r), src, bufs[3].at[r - 1], pairs[2], r, device(self.at, axes[1], to))

    def to_third(self, i):
        axes, (na, nb, nc, per_core, n_a, n_b), bufs, pairs = self.parts(i)
        total = bufs[2][pl.ds(self.at[axes[1]] * n_b, n_b)]
        for r in range(1, nb):
            self.took("b", i, r)
            total = total + bufs[3][r - 1]
        me = self.at[axes[2]]
        bufs[4][me] = total
        for r in away(nc):
            who = device(self.at, axes[2], (me + r) % nc)
            self.copy(("c", i, r), bufs[4].at[me], bufs[4].at[me], pairs[3], r, who)

    def back_second(self, i):
        axes, (na, nb, nc, per_core, n_a, n_b), bufs, pairs = self.parts(i)
        for r in range(1, nc):
            self.took("c", i, r)
        total = bufs[4][0]
        for k in range(1, nc):
            total = total + bufs[4][k]
        me = self.at[axes[1]]
        mine = pl.ds(me * n_b, n_b)
        bufs[5][mine] = (total * self.scale).astype(BF16)
        for r in away(nb):
            who = device(self.at, axes[1], (me + r) % nb)
            self.copy(("d", i, r), bufs[5].at[mine], bufs[5].at[mine], pairs[4], r, who)

    def back_first(self, i):
        axes, (na, nb, nc, per_core, n_a, n_b), bufs, pairs = self.parts(i)
        for r in range(1, nb):
            self.took("d", i, r)
        mine = self.chunk(i, self.at["c"], 0)
        whole = bufs[5].at[pl.ds(0, n_a)]
        for r in away(na):
            who = device(self.at, axes[0], (self.at[axes[0]] + r) % na)
            self.copy(("e", i, r), whole, self.result.at[mine], pairs[5], r, who)
        self.copy(("f", i, 0), whole, self.result.at[mine], pairs[6], 0, self.sibling)
        self.result[mine] = bufs[5][pl.ds(0, n_a)]

    def back_core(self, i, r):
        axes, (na, *_), bufs, pairs = self.parts(i)
        self.took("e", i, r)
        came = self.result.at[self.chunk(i, self.at["c"], na - r)]
        self.copy(("f", i, r), came, came, pairs[6], r, self.sibling)

    def end(self):
        for i in range(len(PARTS)):
            for r in self.rounds(i):
                self.took("f", i, r)
        for made in self.sends:
            made.wait_send()


def step_kernel(
    scale,
    dest_hbm,
    features_hbm,
    place_hbm,
    grad_hbm,
    weight_hbm,
    result_ref,
    rows_ref,
    output_ref,
    dest_ref,
    features_ref,
    place_ref,
    grad_ref,
    weight_ref,
    terms_ref,
    out,
    came,
    back_out,
    back_came,
    face,
    edge,
    select_ref,
    take_ref,
    cells_f,
    cells_g,
    load_sems,
    sems,
    back_sems,
    send_sems,
    recv_sems,
    *scratch,
):
    g, b = lax.axis_index("grp"), lax.axis_index("blk")
    at = coords()
    pairs = (
        (dest_hbm, dest_ref),
        (features_hbm, features_ref),
        (place_hbm, place_ref),
        (grad_hbm, grad_ref),
        (weight_hbm, weight_ref),
    )
    loads = [pltpu.make_async_copy(src, dst, load_sems.at[k]) for k, (src, dst) in enumerate(pairs)]
    for load in loads:
        load.start()
    barrier = pltpu.get_barrier_semaphore()
    greet_block(barrier, g, b)
    for dx in (-1, 1):
        for dy in (-1, 0, 1):
            who = ((g + dx + GRP) % GRP, (b + dy + BLK) % BLK)
            pl.semaphore_signal(barrier, inc=1, device_id=who, device_id_type=MESH)
    for r in range(1, 4):
        who = device(at, "x", (at["x"] + r) % 4)
        pl.semaphore_signal(barrier, inc=1, device_id=who, device_id_type=MESH)

    loads[0].wait()
    slot = row_slots(dest_ref[...], False)
    half = iota((SLOTS, ROWS), 0)
    first, second = half == slot, half == slot + 4
    loads[1].wait()
    ones = jnp.ones((ROWS, 128), BF16)
    packed = dot(one(first), jnp.concatenate([features_ref[:, :128], ones], axis=1))
    packed = packed + dot(one(second), jnp.concatenate([features_ref[:, 128:], ones], axis=1))
    out[...] = jnp.where(packed[:, 128:] > 0.5, packed[:, :128], jnp.inf).reshape(BLK, 8, 128).astype(BF16)
    pl.semaphore_wait(barrier, BLK - 1 + 6 + 3)
    start_all_to_all(g, b, out, came, sems)
    came[b] = out[b]

    loads[2].wait()
    places = jnp.broadcast_to(place_ref[...], (8, VOX)).astype(F32).astype(BF16)
    place8 = dot(places, spread((VOX, SLOTS), 0))[0:1].astype(jnp.int32)
    hits = iota((VOX, SLOTS), 0) == inner(place8)
    low = (iota((VOX, SLOTS), 1) & 4) == 0
    low_hits, high_hits = one(hits & low), one(hits & ~low)
    loads[3].wait()
    grad = dot(one(inner(iota((VOX, VOX), 1)) == iota((VOX, VOX), 0)), grad_ref[...])
    face_of = one(face_source(iota((HALO, VOX), 0)) == iota((HALO, VOX), 1))
    for y in range(3):
        select_ref[y] = one(cell_source(iota((320, 1), 0), y) == iota((320, VOX + HALO), 1))
    back_slot, half = row_slots(dest_ref[...], True), iota((ROWS, SLOTS), 1)
    take_ref[0] = one(half == back_slot)
    take_ref[1] = one(half == back_slot + 4)
    for ref in (cells_f, cells_g):
        for y in range(3):
            for z in (0, 5):
                ref[y, z] = jnp.zeros(ref.shape[2:], F32)
    loads[4].wait()

    end_all_to_all(g, b, out, came, sems)
    got = came[...].astype(F32).reshape(SLOTS, 128)
    there = got < jnp.inf
    rows = jnp.where(there, got, 0.0).astype(BF16)
    both = dot(low_hits, jnp.concatenate([rows, one(there)], axis=1))
    left, occupied = both[:, :128].astype(BF16), both[:, 128:]
    right = dot(high_hits, rows).astype(BF16)
    masked = (grad * occupied).astype(BF16)
    cells = jnp.concatenate([left, right, masked], axis=1)
    face[...] = dot(face_of, cells).reshape(HALO // 8, 8, 384).astype(BF16)
    copies = []
    for k, ((place, size), (dx, dy)) in enumerate(zip(BLOCKS, SIDES)):
        opposite = SIDES.index((-dx, -dy))
        made = pltpu.make_async_remote_copy(
            src_ref=face.at[pl.ds(place, size)],
            dst_ref=edge.at[pl.ds(BLOCKS[opposite][0], size)],
            send_sem=send_sems.at[k],
            recv_sem=recv_sems.at[k],
            device_id=((g + dx + GRP) % GRP, (b + dy + BLK) % BLK),
            device_id_type=MESH,
        )
        made.start()
        copies.append(made)
    row = iota((HALO, 1), 0)
    corner = (row - 128) >> 3
    on_x = (row < 64) | (row >= 128)
    on_y = row >= 64
    x_far = jnp.where(row < 64, row >> 5, corner >> 1)
    y_far = jnp.where(row < 128, (row - 64) >> 5, corner & 1)
    at_x = jnp.where(x_far == 1, jnp.where(g == GRP - 1, 1, 0), jnp.where(g == 0, 1, 0))
    at_y = jnp.where(y_far == 1, jnp.where(b == BLK - 1, 1, 0), jnp.where(b == 0, 1, 0))
    beyond = (on_x & (at_x == 1)) | (on_y & (at_y == 1))
    turned = jnp.concatenate([left, right], axis=1).astype(F32).T.astype(BF16)
    for y in range(3):
        cells_g[y, 1:5] = dot(select_ref[y, :, :VOX], masked).reshape(4, 10, 8, 128)
    for made in copies:
        made.wait()
    halo = jnp.where(beyond, 0.0, edge[...].astype(F32).reshape(HALO, 384)).astype(BF16)
    for y in range(3):
        outer = dot(select_ref[y, :, VOX:], halo[:, 256:]).reshape(4, 10, 8, 128)
        cells_g[y, 1:5] = cells_g[y, 1:5] + outer

    def window(ref, x, y, z):
        part = ref[y, z : z + 4, x : x + 8]
        return part.reshape(VOX, part.shape[-1]).astype(BF16)

    def seen(group):
        x, y = group // 3, group % 3
        return jnp.concatenate([window(cells_g, 2 - x, 2 - y, 2 - z) for z in range(3)], axis=1)

    def near(group):
        x, y = group // 3, group % 3
        return jnp.concatenate([window(cells_f, x, y, z) for z in range(3)], axis=1)

    def contribute(groups):
        for group in groups:
            terms = dot(turned, seen(group))
            for z in range(3):
                k = group * 3 + z
                terms_ref[k * 32 : (k + 1) * 32] = terms[:, z * 128 : (z + 1) * 128].reshape(32, 8, 128)

    summed = Reduction(at, scale, terms_ref, result_ref, scratch)
    contribute((4, 5, 6))
    summed.to_core(2)
    contribute((7, 8))
    summed.to_core(3)
    summed.to_first(2)
    contribute((3, 2))
    summed.to_core(1)
    summed.to_first(3)
    contribute((1, 0))
    summed.to_core(0)
    summed.to_first(1)
    summed.to_first(0)

    data = jnp.concatenate([cells[:, :256], halo[:, :256]], axis=0)
    for y in range(3):
        cells_f[y, 1:5] = dot(select_ref[y], data).reshape(4, 10, 8, 256)
    total = jnp.zeros((VOX, 128), F32)
    back = jnp.zeros((VOX, 256), F32)
    for group in range(9):
        weights = [weight_ref[group * 3 + z] for z in range(3)]
        back = back + dot(seen(group), jnp.concatenate(weights, axis=1), ((1,), (1,)))
        total = total + dot(near(group), jnp.concatenate(weights, axis=0))
    natural = one(inner(iota((VOX, VOX), 0)) == iota((VOX, VOX), 1))
    output_ref[...] = dot(natural, (total * occupied).astype(BF16)).astype(BF16)
    grid_l = (back[:, :128] * occupied).astype(BF16)
    grid_r = (back[:, 128:] * occupied).astype(BF16)
    returned = dot(low_hits, grid_l, ((0,), (0,))) + dot(high_hits, grid_r, ((0,), (0,)))
    back_out[...] = returned.reshape(BLK, 8, 128).astype(BF16)

    order = (1, 2, 3, 0)
    for i in order:
        summed.to_second(i)
    for i in order:
        summed.to_third(i)
    start_all_to_all(g, b, back_out, back_came, back_sems)
    back_came[b] = back_out[b]
    for i in order:
        summed.back_second(i)
    for i in order:
        summed.back_first(i)
    end_all_to_all(g, b, back_out, back_came, back_sems)
    rows = back_came[...].astype(F32).reshape(SLOTS, 128).astype(BF16)
    rows_ref[:, :128] = dot(take_ref[0], rows).astype(BF16)
    rows_ref[:, 128:] = dot(take_ref[1], rows).astype(BF16)
    for r in range(1, 8):
        for i in order:
            if r < part_sizes(PARTS[i])[0]:
                summed.back_core(i, r)
    summed.end()


def store_kernel(*refs):
    count = len(refs) // 2
    sems = refs[-1]
    copies = [pltpu.make_async_copy(refs[k], refs[count + k], sems.at[k]) for k in range(count)]
    for made in copies:
        made.start()
    for made in copies:
        made.wait()


def store(arrays):
    vmem, hbm = pl.BlockSpec(memory_space=pltpu.VMEM), pl.BlockSpec(memory_space=pltpu.HBM)
    return pl.pallas_call(
        store_kernel,
        out_shape=[jax.ShapeDtypeStruct(a.shape, a.dtype) for a in arrays],
        in_specs=[vmem] * len(arrays),
        out_specs=[hbm] * len(arrays),
        scratch_shapes=[pltpu.SemaphoreType.DMA((len(arrays),))],
        name="store",
        compiler_params=pltpu.CompilerParams(vmem_limit_bytes=8 << 20),
    )(*arrays)


def shards(features, dest, placement, weight, grad_out):
    count = ROWS * lax.axis_size("grp") * lax.axis_size("blk")
    vmem, hbm = pl.BlockSpec(memory_space=pltpu.VMEM), pl.BlockSpec(memory_space=pltpu.HBM)
    tiles = pltpu.VMEM((BLK, 8, 128), BF16)
    inputs = (dest.reshape(1, ROWS), features, placement, grad_out.reshape(VOX, 128), weight)
    weight_grad, grad_rows, output = pl.pallas_call(
        lambda *refs: step_kernel(1.0 / math.sqrt(count), *refs),
        out_shape=(
            jax.ShapeDtypeStruct((864, 8, 128), BF16),
            jax.ShapeDtypeStruct((ROWS, 256), BF16),
            jax.ShapeDtypeStruct((VOX, 128), BF16),
        ),
        in_specs=[hbm] * 5,
        out_specs=(vmem,) * 3,
        scratch_shapes=[
            pltpu.VMEM((1, ROWS), jnp.int32),
            pltpu.VMEM((ROWS, 256), BF16),
            pltpu.VMEM((1, VOX), jnp.int32),
            pltpu.VMEM((VOX, 128), BF16),
            pltpu.VMEM((27, 256, 128), BF16),
            pltpu.VMEM((864, 8, 128), F32),
            tiles,
            tiles,
            tiles,
            tiles,
            pltpu.VMEM((HALO // 8, 8, 384), BF16),
            pltpu.VMEM((HALO // 8, 8, 384), BF16),
            pltpu.VMEM((3, 320, VOX + HALO), BF16),
            pltpu.VMEM((2, ROWS, SLOTS), BF16),
            pltpu.VMEM((3, 6, 10, 8, 256), F32),
            pltpu.VMEM((3, 6, 10, 8, 128), F32),
            pltpu.SemaphoreType.DMA((5,)),
            pltpu.SemaphoreType.DMA((2,)),
            pltpu.SemaphoreType.DMA((2,)),
            pltpu.SemaphoreType.DMA((8,)),
            pltpu.SemaphoreType.DMA((8,)),
        ]
        + reduce_scratch(),
        name="step",
        compiler_params=pltpu.CompilerParams(collective_id=1, has_side_effects=True, vmem_limit_bytes=54_000_000),
    )(*(pltpu.with_memory_space_constraint(a, pltpu.HBM) for a in inputs))
    weight_grad, grad_rows, output = store((weight_grad, grad_rows, output))
    return output.reshape(grad_out.shape), grad_rows, weight_grad.reshape(weight.shape)


def solution(mesh):
    in_specs = (
        P(("grp", "blk"), None),
        P(("grp", "blk"), None),
        P(("grp", "blk"), None),
        P(),
        P("grp", "blk", None, None),
    )
    out_specs = (P("grp", "blk", None, None), P(("grp", "blk"), None), P())
    return jax.shard_map(shards, mesh=mesh, in_specs=in_specs, out_specs=out_specs, check_vma=False)
```

```python
import math

import jax
import jax.numpy as jnp
from jax import lax
from jax.experimental import pallas as pl
from jax.experimental.pallas import tpu as pltpu
from jax.sharding import PartitionSpec as P

MESH = pl.DeviceIdType.MESH
F32, BF16 = jnp.float32, jnp.bfloat16
SIZES = {"x": 4, "y": 8, "z": 8}
PARTS = ((0, 6, "xyz"), (6, 7, "xzy"), (13, 7, "yzx"), (20, 7, "zyx"))
TILE = (8, 128)


VOX, SLOTS, ROWS = 256, 512, 128
GRP, BLK = 8, 64
HALO = 160
BLOCKS = ((0, 4), (4, 4), (8, 4), (12, 4), (16, 1), (17, 1), (18, 1), (19, 1))
SIDES = ((-1, 0), (1, 0), (0, -1), (0, 1), (-1, -1), (-1, 1), (1, -1), (1, 1))


def iota(shape, dim):
    return lax.broadcasted_iota(jnp.int32, shape, dim)


def dot(a, b, dims=((1,), (0,))):
    return lax.dot_general(a, b, (dims, ((), ())), preferred_element_type=F32)


def one(mask):
    return jnp.where(mask, 1.0, 0.0).astype(BF16)


def inner(v):
    return (v & 3) * 64 + (v >> 5) * 8 + ((v >> 2) & 7)


def part_sizes(part):
    first, count, axes = part
    na, nb, nc = (SIZES[a] for a in axes)
    per_core = count * 32 // 2
    n_a = per_core // na
    n_b = -(-n_a // nb)
    return na, nb, nc, per_core, n_a, n_b


def reduce_scratch():
    shapes = []
    for part in PARTS:
        na, nb, nc, per_core, n_a, n_b = part_sizes(part)
        shapes += [
            pltpu.VMEM((na, n_a) + TILE, F32),
            pltpu.VMEM((na - 1, n_a) + TILE, F32),
            pltpu.VMEM((nb * n_b,) + TILE, F32),
            pltpu.VMEM((nb - 1, n_b) + TILE, F32),
            pltpu.VMEM((nc, n_b) + TILE, F32),
            pltpu.VMEM((nb * n_b,) + TILE, BF16),
        ]
        for n in (na, na, nb, nc, nb, na, na):
            shapes += [pltpu.SemaphoreType.DMA((n,)), pltpu.SemaphoreType.DMA((n,))]
    return shapes


PER_PART = 6 + 14


def coords():
    g, b = lax.axis_index("grp"), lax.axis_index("blk")
    return {"x": g // 2, "c": g % 2, "y": b // 8, "z": b % 8}


def device(at, axis, value):
    at = dict(at)
    at[axis] = value
    return (at["x"] * 2 + at["c"], at["y"] * 8 + at["z"])


def row_slots(dest_row, by_row):
    turned = jnp.broadcast_to(dest_row, (ROWS, ROWS))
    wide = turned.astype(F32).T.astype(jnp.int32)
    i, j = iota((ROWS, ROWS), 0), iota((ROWS, ROWS), 1)
    same = wide == turned
    if by_row:
        rank = jnp.sum(jnp.where(same & (j < i), 1.0, 0.0), axis=1, keepdims=True)
        return wide[:, 0:1] * 8 + rank.astype(jnp.int32)
    rank = jnp.sum(jnp.where(same & (i < j), 1.0, 0.0), axis=0, keepdims=True)
    return dest_row * 8 + rank.astype(jnp.int32)


def spread(shape, slot_dim):
    slot, half = iota(shape, slot_dim), iota(shape, 1 - slot_dim)
    return one((half >> 3) * 4 + (half & 3) == slot)


def face_source(row):
    t = row & 31
    far = jnp.where((row & 32) != 0, 7, 0)
    x_side = (t >> 3) * 64 + far * 8 + (t & 7)
    y_side = (t >> 3) * 64 + (t & 7) * 8 + far
    k = (row - 128) >> 3
    corner = (row & 3) * 64 + (k >> 1) * 56 + (k & 1) * 7
    return jnp.where(row < 64, x_side, jnp.where(row < 128, y_side, corner))


def cell_source(row, shift_y):
    z = row // 80
    x = (row >> 3) - z * 10 - 1
    y = (row & 7) + (shift_y - 1)
    in_x, in_y = (x >= 0) & (x < 8), (y >= 0) & (y < 8)
    right, top = jnp.where(x > 7, 1, 0), jnp.where(y > 7, 1, 0)
    inside = z * 64 + x * 8 + y
    x_side = VOX + right * 32 + z * 8 + y
    y_side = VOX + 64 + top * 32 + z * 8 + x
    corner = VOX + 128 + right * 16 + top * 8 + z
    return jnp.where(in_x & in_y, inside, jnp.where(in_y, x_side, jnp.where(in_x, y_side, corner)))


def greet_block(barrier, g, b):
    def signal(r, _):
        pl.semaphore_signal(barrier, inc=1, device_id=(g, (b + r) % BLK), device_id_type=MESH)
        return 0

    lax.fori_loop(1, BLK, signal, 0)


def far_first(i):
    return 4 + i // 2 - i % 2 * (i // 2 * 2 + 1)


def start_all_to_all(g, b, out_ref, in_ref, sems):
    def send(i, _):
        to = (b // 8 + far_first(i // 8)) % 8 * 8 + (b % 8 + far_first(i % 8)) % 8
        pltpu.make_async_remote_copy(
            src_ref=out_ref.at[to],
            dst_ref=in_ref.at[b],
            send_sem=sems.at[0],
            recv_sem=sems.at[1],
            device_id=(g, to),
            device_id_type=MESH,
        ).start()
        return 0

    lax.fori_loop(0, BLK - 1, send, 0)


def end_all_to_all(g, b, out_ref, in_ref, sems):
    pltpu.make_async_remote_copy(
        src_ref=out_ref.at[pl.ds(0, BLK - 1)],
        dst_ref=in_ref.at[pl.ds(0, BLK - 1)],
        send_sem=sems.at[0],
        recv_sem=sems.at[1],
        device_id=(g, (b + 1) % BLK),
        device_id_type=MESH,
    ).wait()


def away(n):
    return sorted(range(1, n), key=lambda r: (-min(r, n - r), r))


class Reduction:
    def __init__(self, at, scale, terms, result, scratch):
        self.at, self.scale, self.terms, self.result = at, scale, terms, result
        self.sibling = device(at, "c", 1 - at["c"])
        self.sends, self.flights = [], {}
        self.own = [scratch[i * PER_PART : (i + 1) * PER_PART] for i in range(len(PARTS))]

    def copy(self, key, src, dst, sems, r, who):
        made = pltpu.make_async_remote_copy(
            src_ref=src, dst_ref=dst, send_sem=sems[0].at[r], recv_sem=sems[1].at[r], device_id=who, device_id_type=MESH
        )
        made.start()
        self.sends.append(made)
        self.flights[key] = made

    def took(self, *key):
        self.flights[key].wait_recv()

    def parts(self, i):
        first, _, axes = PARTS[i]
        bufs, sems = self.own[i][:6], self.own[i][6:]
        pairs = [sems[k : k + 2] for k in range(0, 14, 2)]
        return axes, part_sizes(PARTS[i]), bufs, pairs

    def chunk(self, i, core, r):
        first, _, axes = PARTS[i]
        na, _, _, per_core, n_a, _ = part_sizes(PARTS[i])
        return pl.ds(first * 32 + core * per_core + (self.at[axes[0]] + r) % na * n_a, n_a)

    def rounds(self, i):
        return [*away(part_sizes(PARTS[i])[0]), 0]

    def to_core(self, i):
        axes, _, bufs, pairs = self.parts(i)
        for r in self.rounds(i):
            src = self.terms.at[self.chunk(i, 1 - self.at["c"], r)]
            self.copy(("core", i, r), src, bufs[0].at[r], pairs[0], r, self.sibling)

    def to_first(self, i):
        axes, (na, *_), bufs, pairs = self.parts(i)
        for r in self.rounds(i):
            self.took("core", i, r)
            bufs[0][r] = bufs[0][r] + self.terms[self.chunk(i, self.at["c"], r)]
            if r:
                who = device(self.at, axes[0], (self.at[axes[0]] + r) % na)
                self.copy(("a", i, r), bufs[0].at[r], bufs[1].at[r - 1], pairs[1], r, who)

    def to_second(self, i):
        axes, (na, nb, nc, per_core, n_a, n_b), bufs, pairs = self.parts(i)
        total = bufs[0][0]
        for r in range(1, na):
            self.took("a", i, r)
            total = total + bufs[1][r - 1]
        bufs[2][pl.ds(0, n_a)] = total
        if n_a < nb * n_b:
            bufs[2][pl.ds(n_a, nb * n_b - n_a)] = jnp.zeros((nb * n_b - n_a,) + TILE, F32)
        for r in away(nb):
            to = (self.at[axes[1]] + r) % nb
            src = bufs[2].at[pl.ds(to * n_b, n_b)]
            self.copy(("b", i, r), src, bufs[3].at[r - 1], pairs[2], r, device(self.at, axes[1], to))

    def to_third(self, i):
        axes, (na, nb, nc, per_core, n_a, n_b), bufs, pairs = self.parts(i)
        total = bufs[2][pl.ds(self.at[axes[1]] * n_b, n_b)]
        for r in range(1, nb):
            self.took("b", i, r)
            total = total + bufs[3][r - 1]
        me = self.at[axes[2]]
        bufs[4][me] = total
        for r in away(nc):
            who = device(self.at, axes[2], (me + r) % nc)
            self.copy(("c", i, r), bufs[4].at[me], bufs[4].at[me], pairs[3], r, who)

    def back_second(self, i):
        axes, (na, nb, nc, per_core, n_a, n_b), bufs, pairs = self.parts(i)
        for r in range(1, nc):
            self.took("c", i, r)
        total = bufs[4][0]
        for k in range(1, nc):
            total = total + bufs[4][k]
        me = self.at[axes[1]]
        mine = pl.ds(me * n_b, n_b)
        bufs[5][mine] = (total * self.scale).astype(BF16)
        for r in away(nb):
            who = device(self.at, axes[1], (me + r) % nb)
            self.copy(("d", i, r), bufs[5].at[mine], bufs[5].at[mine], pairs[4], r, who)

    def back_first(self, i):
        axes, (na, nb, nc, per_core, n_a, n_b), bufs, pairs = self.parts(i)
        for r in range(1, nb):
            self.took("d", i, r)
        mine = self.chunk(i, self.at["c"], 0)
        whole = bufs[5].at[pl.ds(0, n_a)]
        for r in away(na):
            who = device(self.at, axes[0], (self.at[axes[0]] + r) % na)
            self.copy(("e", i, r), whole, self.result.at[mine], pairs[5], r, who)
        self.copy(("f", i, 0), whole, self.result.at[mine], pairs[6], 0, self.sibling)
        self.result[mine] = bufs[5][pl.ds(0, n_a)]

    def back_core(self, i, r):
        axes, (na, *_), bufs, pairs = self.parts(i)
        self.took("e", i, r)
        came = self.result.at[self.chunk(i, self.at["c"], na - r)]
        self.copy(("f", i, r), came, came, pairs[6], r, self.sibling)

    def end(self):
        for i in range(len(PARTS)):
            for r in self.rounds(i):
                self.took("f", i, r)
        for made in self.sends:
            made.wait_send()


def step_kernel(
    scale,
    dest_hbm,
    features_hbm,
    place_hbm,
    grad_hbm,
    weight_hbm,
    result_ref,
    rows_ref,
    output_ref,
    dest_ref,
    features_ref,
    place_ref,
    grad_ref,
    weight_ref,
    terms_ref,
    out,
    came,
    back_out,
    back_came,
    face,
    edge,
    select_ref,
    take_ref,
    cells_f,
    cells_g,
    load_sems,
    sems,
    back_sems,
    send_sems,
    recv_sems,
    *scratch,
):
    g, b = lax.axis_index("grp"), lax.axis_index("blk")
    at = coords()
    pairs = (
        (dest_hbm, dest_ref),
        (features_hbm, features_ref),
        (place_hbm, place_ref),
        (grad_hbm, grad_ref),
        (weight_hbm, weight_ref),
    )
    loads = [pltpu.make_async_copy(src, dst, load_sems.at[k]) for k, (src, dst) in enumerate(pairs)]
    for load in loads:
        load.start()
    barrier = pltpu.get_barrier_semaphore()
    greet_block(barrier, g, b)
    for dx in (-1, 1):
        for dy in (-1, 0, 1):
            who = ((g + dx + GRP) % GRP, (b + dy + BLK) % BLK)
            pl.semaphore_signal(barrier, inc=1, device_id=who, device_id_type=MESH)
    for r in range(1, 4):
        who = device(at, "x", (at["x"] + r) % 4)
        pl.semaphore_signal(barrier, inc=1, device_id=who, device_id_type=MESH)

    loads[0].wait()
    slot = row_slots(dest_ref[...], False)
    half = iota((SLOTS, ROWS), 0)
    first, second = half == slot, half == slot + 4
    loads[1].wait()
    ones = jnp.ones((ROWS, 128), BF16)
    packed = dot(one(first), jnp.concatenate([features_ref[:, :128], ones], axis=1))
    packed = packed + dot(one(second), jnp.concatenate([features_ref[:, 128:], ones], axis=1))
    out[...] = jnp.where(packed[:, 128:] > 0.5, packed[:, :128], jnp.inf).reshape(BLK, 8, 128).astype(BF16)
    pl.semaphore_wait(barrier, BLK - 1 + 6 + 3)
    start_all_to_all(g, b, out, came, sems)
    came[b] = out[b]

    loads[2].wait()
    places = jnp.broadcast_to(place_ref[...], (8, VOX)).astype(F32).astype(BF16)
    place8 = dot(places, spread((VOX, SLOTS), 0))[0:1].astype(jnp.int32)
    hits = iota((VOX, SLOTS), 0) == inner(place8)
    low = (iota((VOX, SLOTS), 1) & 4) == 0
    low_hits, high_hits = one(hits & low), one(hits & ~low)
    loads[3].wait()
    grad = dot(one(inner(iota((VOX, VOX), 1)) == iota((VOX, VOX), 0)), grad_ref[...])
    face_of = one(face_source(iota((HALO, VOX), 0)) == iota((HALO, VOX), 1))
    for y in range(3):
        select_ref[y] = one(cell_source(iota((320, 1), 0), y) == iota((320, VOX + HALO), 1))
    back_slot, half = row_slots(dest_ref[...], True), iota((ROWS, SLOTS), 1)
    take_ref[0] = one(half == back_slot)
    take_ref[1] = one(half == back_slot + 4)
    for ref in (cells_f, cells_g):
        for y in range(3):
            for z in (0, 5):
                ref[y, z] = jnp.zeros(ref.shape[2:], F32)
    loads[4].wait()

    end_all_to_all(g, b, out, came, sems)
    got = came[...].astype(F32).reshape(SLOTS, 128)
    there = got < jnp.inf
    rows = jnp.where(there, got, 0.0).astype(BF16)
    both = dot(low_hits, jnp.concatenate([rows, one(there)], axis=1))
    left, occupied = both[:, :128].astype(BF16), both[:, 128:]
    right = dot(high_hits, rows).astype(BF16)
    masked = (grad * occupied).astype(BF16)
    cells = jnp.concatenate([left, right, masked], axis=1)
    face[...] = dot(face_of, cells).reshape(HALO // 8, 8, 384).astype(BF16)
    copies = []
    for k, ((place, size), (dx, dy)) in enumerate(zip(BLOCKS, SIDES)):
        opposite = SIDES.index((-dx, -dy))
        made = pltpu.make_async_remote_copy(
            src_ref=face.at[pl.ds(place, size)],
            dst_ref=edge.at[pl.ds(BLOCKS[opposite][0], size)],
            send_sem=send_sems.at[k],
            recv_sem=recv_sems.at[k],
            device_id=((g + dx + GRP) % GRP, (b + dy + BLK) % BLK),
            device_id_type=MESH,
        )
        made.start()
        copies.append(made)
    row = iota((HALO, 1), 0)
    corner = (row - 128) >> 3
    on_x = (row < 64) | (row >= 128)
    on_y = row >= 64
    x_far = jnp.where(row < 64, row >> 5, corner >> 1)
    y_far = jnp.where(row < 128, (row - 64) >> 5, corner & 1)
    at_x = jnp.where(x_far == 1, jnp.where(g == GRP - 1, 1, 0), jnp.where(g == 0, 1, 0))
    at_y = jnp.where(y_far == 1, jnp.where(b == BLK - 1, 1, 0), jnp.where(b == 0, 1, 0))
    beyond = (on_x & (at_x == 1)) | (on_y & (at_y == 1))
    turned = jnp.concatenate([left, right], axis=1).astype(F32).T.astype(BF16)
    for y in range(3):
        cells_g[y, 1:5] = dot(select_ref[y, :, :VOX], masked).reshape(4, 10, 8, 128)
    for made in copies:
        made.wait()
    halo = jnp.where(beyond, 0.0, edge[...].astype(F32).reshape(HALO, 384)).astype(BF16)
    for y in range(3):
        outer = dot(select_ref[y, :, VOX:], halo[:, 256:]).reshape(4, 10, 8, 128)
        cells_g[y, 1:5] = cells_g[y, 1:5] + outer

    def window(ref, x, y, z):
        part = ref[y, z : z + 4, x : x + 8]
        return part.reshape(VOX, part.shape[-1]).astype(BF16)

    def seen(group):
        x, y = group // 3, group % 3
        return jnp.concatenate([window(cells_g, 2 - x, 2 - y, 2 - z) for z in range(3)], axis=1)

    def near(group):
        x, y = group // 3, group % 3
        return jnp.concatenate([window(cells_f, x, y, z) for z in range(3)], axis=1)

    def contribute(groups):
        for group in groups:
            terms = dot(turned, seen(group))
            for z in range(3):
                k = group * 3 + z
                terms_ref[k * 32 : (k + 1) * 32] = terms[:, z * 128 : (z + 1) * 128].reshape(32, 8, 128)

    summed = Reduction(at, scale, terms_ref, result_ref, scratch)
    contribute((4, 5, 6))
    summed.to_core(2)
    contribute((7, 8))
    summed.to_core(3)
    summed.to_first(2)
    contribute((3, 2))
    summed.to_core(1)
    summed.to_first(3)
    contribute((1, 0))
    summed.to_core(0)
    summed.to_first(1)
    summed.to_first(0)

    data = jnp.concatenate([cells[:, :256], halo[:, :256]], axis=0)
    for y in range(3):
        cells_f[y, 1:5] = dot(select_ref[y], data).reshape(4, 10, 8, 256)
    total = jnp.zeros((VOX, 128), F32)
    back = jnp.zeros((VOX, 256), F32)
    for group in range(9):
        weights = [weight_ref[group * 3 + z] for z in range(3)]
        back = back + dot(seen(group), jnp.concatenate(weights, axis=1), ((1,), (1,)))
        total = total + dot(near(group), jnp.concatenate(weights, axis=0))
    natural = one(inner(iota((VOX, VOX), 0)) == iota((VOX, VOX), 1))
    output_ref[...] = dot(natural, (total * occupied).astype(BF16)).astype(BF16)
    grid_l = (back[:, :128] * occupied).astype(BF16)
    grid_r = (back[:, 128:] * occupied).astype(BF16)
    returned = dot(low_hits, grid_l, ((0,), (0,))) + dot(high_hits, grid_r, ((0,), (0,)))
    back_out[...] = returned.reshape(BLK, 8, 128).astype(BF16)

    order = (2, 3, 1, 0)
    for i in order:
        summed.to_second(i)
    for i in order:
        summed.to_third(i)
    start_all_to_all(g, b, back_out, back_came, back_sems)
    back_came[b] = back_out[b]
    for i in order:
        summed.back_second(i)
    for i in order:
        summed.back_first(i)
    end_all_to_all(g, b, back_out, back_came, back_sems)
    rows = back_came[...].astype(F32).reshape(SLOTS, 128).astype(BF16)
    rows_ref[:, :128] = dot(take_ref[0], rows).astype(BF16)
    rows_ref[:, 128:] = dot(take_ref[1], rows).astype(BF16)
    for r in range(1, 8):
        for i in order:
            if r < part_sizes(PARTS[i])[0]:
                summed.back_core(i, r)
    summed.end()


def store_kernel(*refs):
    count = len(refs) // 2
    sems = refs[-1]
    copies = [pltpu.make_async_copy(refs[k], refs[count + k], sems.at[k]) for k in range(count)]
    for made in copies:
        made.start()
    for made in copies:
        made.wait()


def store(arrays):
    vmem, hbm = pl.BlockSpec(memory_space=pltpu.VMEM), pl.BlockSpec(memory_space=pltpu.HBM)
    return pl.pallas_call(
        store_kernel,
        out_shape=[jax.ShapeDtypeStruct(a.shape, a.dtype) for a in arrays],
        in_specs=[vmem] * len(arrays),
        out_specs=[hbm] * len(arrays),
        scratch_shapes=[pltpu.SemaphoreType.DMA((len(arrays),))],
        name="store",
        compiler_params=pltpu.CompilerParams(vmem_limit_bytes=8 << 20),
    )(*arrays)


def shards(features, dest, placement, weight, grad_out):
    count = ROWS * lax.axis_size("grp") * lax.axis_size("blk")
    vmem, hbm = pl.BlockSpec(memory_space=pltpu.VMEM), pl.BlockSpec(memory_space=pltpu.HBM)
    tiles = pltpu.VMEM((BLK, 8, 128), BF16)
    inputs = (dest.reshape(1, ROWS), features, placement, grad_out.reshape(VOX, 128), weight)
    weight_grad, grad_rows, output = pl.pallas_call(
        lambda *refs: step_kernel(1.0 / math.sqrt(count), *refs),
        out_shape=(
            jax.ShapeDtypeStruct((864, 8, 128), BF16),
            jax.ShapeDtypeStruct((ROWS, 256), BF16),
            jax.ShapeDtypeStruct((VOX, 128), BF16),
        ),
        in_specs=[hbm] * 5,
        out_specs=(vmem,) * 3,
        scratch_shapes=[
            pltpu.VMEM((1, ROWS), jnp.int32),
            pltpu.VMEM((ROWS, 256), BF16),
            pltpu.VMEM((1, VOX), jnp.int32),
            pltpu.VMEM((VOX, 128), BF16),
            pltpu.VMEM((27, 256, 128), BF16),
            pltpu.VMEM((864, 8, 128), F32),
            tiles,
            tiles,
            tiles,
            tiles,
            pltpu.VMEM((HALO // 8, 8, 384), BF16),
            pltpu.VMEM((HALO // 8, 8, 384), BF16),
            pltpu.VMEM((3, 320, VOX + HALO), BF16),
            pltpu.VMEM((2, ROWS, SLOTS), BF16),
            pltpu.VMEM((3, 6, 10, 8, 256), F32),
            pltpu.VMEM((3, 6, 10, 8, 128), F32),
            pltpu.SemaphoreType.DMA((5,)),
            pltpu.SemaphoreType.DMA((2,)),
            pltpu.SemaphoreType.DMA((2,)),
            pltpu.SemaphoreType.DMA((8,)),
            pltpu.SemaphoreType.DMA((8,)),
        ]
        + reduce_scratch(),
        name="step",
        compiler_params=pltpu.CompilerParams(collective_id=1, has_side_effects=True, vmem_limit_bytes=54_000_000),
    )(*(pltpu.with_memory_space_constraint(a, pltpu.HBM) for a in inputs))
    weight_grad, grad_rows, output = store((weight_grad, grad_rows, output))
    return output.reshape(grad_out.shape), grad_rows, weight_grad.reshape(weight.shape)


def solution(mesh):
    in_specs = (
        P(("grp", "blk"), None),
        P(("grp", "blk"), None),
        P(("grp", "blk"), None),
        P(),
        P("grp", "blk", None, None),
    )
    out_specs = (P("grp", "blk", None, None), P(("grp", "blk"), None), P())
    return jax.shard_map(shards, mesh=mesh, in_specs=in_specs, out_specs=out_specs, check_vma=False)
```
